32 devices in a mesh: dp: 16 (over z, y, core), fsdp: 2 (over x).
Axes of the slice: x: 2, y: 2, z: 4, core: 2. Of those that a mesh axis runs over, the one named last changes fastest.
Arguments:
- inputs: bfloat16 [64, 640, 768], P(('dp', 'fsdp')), may hold values from -6 to 6
- segments: int32 [64, 640], P(('dp', 'fsdp')), may hold values from 0 to 3, as said below
- query_wordword: bfloat16 [768, 768], P('fsdp'), may hold values from -0.21875 to 0.21875
- query_wordent: bfloat16 [768, 768], P('fsdp'), may hold values from -0.21875 to 0.21875
- query_entword: bfloat16 [768, 768], P('fsdp'), may hold values from -0.21875 to 0.21875
- query_entent: bfloat16 [768, 768], P('fsdp'), may hold values from -0.21875 to 0.21875
- bias_wordword: bfloat16 [768], P('fsdp'), may hold values from -3 to 3
- bias_wordent: bfloat16 [768], P('fsdp'), may hold values from -3 to 3
- bias_entword: bfloat16 [768], P('fsdp'), may hold values from -3 to 3
- bias_entent: bfloat16 [768], P('fsdp'), may hold values from -3 to 3
- key_weight: bfloat16 [768, 768], P('fsdp'), may hold values from -0.21875 to 0.21875
- value_weight: bfloat16 [768, 768], P('fsdp'), may hold values from -0.21875 to 0.21875
- value_bias: bfloat16 [768], P('fsdp'), may hold values from -3 to 3
- out_weight: bfloat16 [768, 768], P('fsdp'), may hold values from -0.875 to 0.875
- out_bias: bfloat16 [768], P('fsdp'), may hold values from -3 to 3
- gain_attn: bfloat16 [768], P('fsdp'), may hold values from 0.099609375 to 1.8984375
- shift_attn: bfloat16 [768], P('fsdp'), may hold values from -3 to 3
- inner_weight: bfloat16 [768, 3072], P('fsdp'), may hold values from -0.21875 to 0.21875
- inner_bias: bfloat16 [3072], P('fsdp'), may hold values from -3 to 3
- down_weight: bfloat16 [3072, 768], P('fsdp'), may hold values from -0.109375 to 0.109375
- down_bias: bfloat16 [768], P('fsdp'), may hold values from -3 to 3
- gain_ffn: bfloat16 [768], P('fsdp'), may hold values from 0.099609375 to 1.8984375
- shift_ffn: bfloat16 [768], P('fsdp'), may hold values from -3 to 3
- cotangent: bfloat16 [64, 640, 768], P(('dp', 'fsdp')), may hold values from -6 to 6
Outputs:
- output: bfloat16 [64, 640, 768], P(('dp', 'fsdp'))
- grad_inputs: float32 [64, 640, 768], P(('dp', 'fsdp'))
- grad_query_wordword: float32 [768, 768], P('fsdp')
- grad_query_wordent: float32 [768, 768], P('fsdp')
- grad_query_entword: float32 [768, 768], P('fsdp')
- grad_query_entent: float32 [768, 768], P('fsdp')
- grad_bias_wordword: float32 [768], P('fsdp')
- grad_bias_wordent: float32 [768], P('fsdp')
- grad_bias_entword: float32 [768], P('fsdp')
- grad_bias_entent: float32 [768], P('fsdp')
- grad_key_weight: float32 [768, 768], P('fsdp')
- grad_value_weight: float32 [768, 768], P('fsdp')
- grad_value_bias: float32 [768], P('fsdp')
- grad_out_weight: float32 [768, 768], P('fsdp')
- grad_out_bias: float32 [768], P('fsdp')
- grad_gain_attn: float32 [768], P('fsdp')
- grad_shift_attn: float32 [768], P('fsdp')
- grad_inner_weight: float32 [768, 3072], P('fsdp')
- grad_inner_bias: float32 [3072], P('fsdp')
- grad_down_weight: float32 [3072, 768], P('fsdp')
- grad_down_bias: float32 [768], P('fsdp')
- grad_gain_ffn: float32 [768], P('fsdp')
- grad_shift_ffn: float32 [768], P('fsdp')
The draws below stay inside these ranges and needn't reach their ends.
Inputs may be any that keep to these rules, and one draw needn't show every extreme that they name: `segments`: in each sequence the segment numbers of the 512 word rows never fall and take every value from 0 to 3; those of the 128 entity rows never fall.
All inputs are finite; a program needn't handle non-finite values.
Results may differ from the reference program's by a relative error of at most 0.02.
Values may be sent and summed in bfloat16 or wider, within the bound.
A program may use at most 256 MiB of HBM per device.

```python
import jax
import jax.numpy as jnp
from jax import lax

D = 768
HEADS = 12
HD = 64
FF = 3072
WORDS = 512
ENTS = 128
DOCS = 4
SEQS = 64


def draw_segments(key, part):
    seq_keys = jax.random.split(key, SEQS)

    def single(one_key):
        key_cuts, key_ents = jax.random.split(one_key)
        borders = jax.random.permutation(key_cuts, WORDS - 1)[:DOCS - 1] + 1
        places = jnp.arange(WORDS, dtype=jnp.int32)
        word_part = jnp.sum((places[:, None] >= borders[None, :]).astype(jnp.int32), axis=1)
        entity_part = jnp.sort(jax.random.randint(key_ents, (ENTS,), 0, DOCS))
        return jnp.concatenate([word_part.astype(jnp.int32), entity_part.astype(jnp.int32)])
    return jax.vmap(single)(seq_keys)


def strengthened(entries, stream_key, source, target, shards_of, factor):
    def block_of(dim):
        return (jnp.arange(entries.shape[dim]) // (entries.shape[dim] // shards_of)).reshape((-1,) + (1,) * (entries.ndim - 1 - dim))

    first = jax.random.permutation(stream_key, shards_of)[block_of(target)]
    other_side = (block_of(target) + shards_of // 2) % shards_of
    return jnp.where((block_of(source) == first) | (block_of(source) == other_side), factor * entries, entries)


def block_levels(stream_key, extent, shards, least, largest):
    def one(position, parts):
        heights = jax.random.uniform(jax.random.fold_in(jax.random.fold_in(stream_key, 6), position), (parts,), jnp.float32, least / len(shards), largest / len(shards))
        return jnp.repeat(jnp.exp(heights), extent[position] // parts).reshape((-1,) + (1,) * (len(extent) - position - 1))

    level = one(*shards[0])
    for cut in shards[1:]:
        level = level * one(*cut)
    return level


def centred(rng, dims, deviation, limit, pieces=(), kind=jnp.bfloat16):
    array = jax.random.normal(rng, dims, jnp.float32) * deviation
    if len(pieces) > 0:
        array = block_levels(rng, dims, pieces, -0.22, 0.18) * array
    return jnp.clip(array, min=-limit, max=limit).astype(kind)


def bell_draw_with(own_key, dims, deviation, most, shards, heavy, kind=jnp.bfloat16):
    entries = deviation * jax.random.normal(own_key, dims, jnp.float32)
    if shards:
        entries = entries * block_levels(own_key, dims, shards, -0.22, 0.18)
    return jnp.clip(strengthened(entries, jax.random.fold_in(own_key, 3), *heavy), -most, most).astype(kind)


def setup_inputs(seed: int = 0) -> dict:
    splits = jax.random.split(jax.random.key(seed), 25)
    return {
        "inputs": bell_draw_with(splits[0], (SEQS, WORDS + ENTS, D), 1.0, 6.0, ((0, 32),), (0, 2, 32, 2.75)),
        "segments": draw_segments(jax.random.fold_in(splits[24], 71), 0),
        "query_wordword": centred(splits[2], (D, D), D ** -0.5, 0.21875, ((0, 2),)),
        "query_wordent": centred(splits[3], (D, D), D ** -0.5, 0.21875, ((0, 2),)),
        "query_entword": centred(splits[4], (D, D), D ** -0.5, 0.21875, ((0, 2),)),
        "query_entent": centred(splits[5], (D, D), D ** -0.5, 0.21875, ((0, 2),)),
        "bias_wordword": centred(splits[6], (D,), 0.5, 3.0, ((0, 2),)),
        "bias_wordent": centred(splits[7], (D,), 0.5, 3.0, ((0, 2),)),
        "bias_entword": centred(splits[8], (D,), 0.5, 3.0, ((0, 2),)),
        "bias_entent": centred(splits[9], (D,), 0.5, 3.0, ((0, 2),)),
        "key_weight": centred(splits[10], (D, D), D ** -0.5, 0.21875, ((0, 2),)),
        "value_weight": centred(splits[11], (D, D), D ** -0.5, 0.21875, ((0, 2),)),
        "value_bias": centred(splits[12], (D,), 0.5, 3.0, ((0, 2),)),
        "out_weight": centred(splits[13], (D, D), (D // 16) ** -0.5, 0.875, ((0, 2),)),
        "out_bias": centred(splits[14], (D,), 0.5, 3.0, ((0, 2),)),
        "gain_attn": jnp.clip(1.0 + 0.18 * jax.random.normal(splits[15], (D,), jnp.float32), 0.099609375, 1.8984375).astype(jnp.bfloat16),
        "shift_attn": centred(splits[16], (D,), 0.5, 3.0, ((0, 2),)),
        "inner_weight": centred(splits[17], (D, FF), D ** -0.5, 0.21875, ((0, 2),)),
        "inner_bias": centred(splits[18], (FF,), 0.5, 3.0, ((0, 2),)),
        "down_weight": centred(splits[19], (FF, D), FF ** -0.5, 0.109375, ((0, 2),)),
        "down_bias": centred(splits[20], (D,), 0.5, 3.0, ((0, 2),)),
        "gain_ffn": jnp.clip(1.0 + 0.18 * jax.random.normal(splits[21], (D,), jnp.float32), 0.099609375, 1.8984375).astype(jnp.bfloat16),
        "shift_ffn": centred(splits[22], (D,), 0.5, 3.0, ((0, 2),)),
        "cotangent": centred(splits[23], (SEQS, WORDS + ENTS, D), 1.0, 6.0, ((0, 32),)),
    }


@jax.custom_vjp
def low(v):
    return lax.optimization_barrier(v.astype(jnp.bfloat16)).astype(jnp.float32)

@jax.custom_vjp
def low_back(v):
    return v

def low_keep(v):
    return (low(v), None)

def low_pass(kept, grad):
    return (grad,)

def back_keep(v):
    return (v, None)

def back_low(kept, grad):
    return (low(grad),)
low.defvjp(low_keep, low_pass)
low_back.defvjp(back_keep, back_low)
norm_eps = 1e-12
highest = lax.Precision.HIGHEST

def matmul(left, right):
    return jnp.dot(left, right, precision=highest)

def layer_norm(values, gain, shift):
    center = values - lax.optimization_barrier(jnp.mean(values, axis=-1, keepdims=True))
    variance = lax.optimization_barrier(jnp.mean(center * center, axis=-1, keepdims=True))
    return center * lax.rsqrt(variance + norm_eps) * gain + shift

def one_sequence(params, item):
    m_wordword, m_wordent, m_entword, m_entent, b_wordword, b_wordent, b_entword, b_entent, m_key, m_value, b_value, m_out, b_out, g_attn, s_attn, m_inner, b_inner, m_down, b_down, g_ffn, s_ffn = params
    seq_rows, seg_ids = item
    length = seq_rows.shape[0]
    word_rows = seq_rows[:WORDS]
    ent_rows = seq_rows[WORDS:]

    def project(source, weight, bias):
        return low(low_back(matmul(source, weight) + bias)).reshape(source.shape[0], HEADS, HD)
    wordword = project(word_rows, m_wordword, b_wordword)
    wordent = project(word_rows, m_wordent, b_wordent)
    entword = project(ent_rows, m_entword, b_entword)
    entent = project(ent_rows, m_entent, b_entent)
    keyset = low(low_back(matmul(seq_rows, m_key))).reshape(length, HEADS, HD)
    valset = low(low_back(matmul(seq_rows, m_value) + b_value)).reshape(length, HEADS, HD)
    key_words = keyset[:WORDS]
    key_ents = keyset[WORDS:]

    def product(query, keys):
        return jnp.einsum('qhd,khd->hqk', query, keys, precision=highest)
    upper_half = jnp.concatenate([product(wordword, key_words), product(wordent, key_ents)], axis=2)
    lower_half = jnp.concatenate([product(entword, key_words), product(entent, key_ents)], axis=2)
    scores = jnp.concatenate([upper_half, lower_half], axis=1) * HD ** (-0.5)
    scores = low_back(scores)
    same = seg_ids[:, None] == seg_ids[None, :]
    scores = jnp.where(same[None], scores, -1000000000.0)
    prob = low(jax.nn.softmax(scores, axis=-1))
    context = jnp.einsum('hqk,khd->qhd', prob, valset, precision=highest).reshape(length, HEADS * HD)
    context = low(low_back(context))
    attended = low_back(matmul(context, m_out) + b_out)
    hidden = layer_norm(seq_rows + attended, g_attn, s_attn)
    upper = low_back(matmul(low(hidden), m_inner) + b_inner)
    active = low(jax.nn.gelu(upper, approximate=False))
    fed = low_back(matmul(active, m_down) + b_down)
    return layer_norm(hidden + fed, g_ffn, s_ffn)

def reference(inputs, segments, query_wordword, query_wordent, query_entword, query_entent, bias_wordword, bias_wordent, bias_entword, bias_entent, key_weight, value_weight, value_bias, out_weight, out_bias, gain_attn, shift_attn, inner_weight, inner_bias, down_weight, down_bias, gain_ffn, shift_ffn, cotangent):
    params = tuple((p.astype(jnp.float32) for p in (query_wordword, query_wordent, query_entword, query_entent, bias_wordword, bias_wordent, bias_entword, bias_entent, key_weight, value_weight, value_bias, out_weight, out_bias, gain_attn, shift_attn, inner_weight, inner_bias, down_weight, down_bias, gain_ffn, shift_ffn)))
    rows = inputs.astype(jnp.float32)
    checked = jax.checkpoint(one_sequence)

    def forward(all_rows, weights):
        return lax.map(lambda item: checked(weights, item), (all_rows, segments))
    result, pull = jax.vjp(forward, rows, params)
    grad_rows, grads = pull(cotangent.astype(jnp.float32))
    return (result.astype(jnp.bfloat16), grad_rows, grads[0], grads[1], grads[2], grads[3], grads[4], grads[5], grads[6], grads[7], grads[8], grads[9], grads[10], grads[11], grads[12], grads[13], grads[14], grads[15], grads[16], grads[17], grads[18], grads[19], grads[20])
```

```python
import functools
import jax
import jax.numpy as jnp
from jax import lax
from jax.experimental import pallas as pl
from jax.experimental.pallas import tpu as pltpu
from jax.sharding import PartitionSpec as P

HD = 64
WORDS = 512
norm_eps = 1e-12
F32 = jnp.float32
BF16 = jnp.bfloat16
MASKED = -1000000000.0


def nn(a, b):
    return lax.dot_general(a, b, (((1,), (0,)), ((), ())), preferred_element_type=F32)


def nt(a, b):
    return lax.dot_general(a, b, (((1,), (1,)), ((), ())), preferred_element_type=F32)


def vmem(mb):
    return pltpu.CompilerParams(vmem_limit_bytes=mb * 1024 * 1024)


def spans(total, size):
    return [(s, min(size, total - s)) for s in range(0, total, size)]


def project_kernel(x, w, b, qw, qe, k, v):
    words = x[0, :WORDS]
    ents = x[0, WORDS:]
    scale = HD ** -0.5

    def query(rows, i):
        return ((nn(rows, w[i]) + b[i:i + 1]).astype(BF16) * scale).astype(BF16)

    qw[0, :WORDS] = query(words, 0)
    qe[0, :WORDS] = query(words, 1)
    qw[0, WORDS:] = query(ents, 2)
    qe[0, WORDS:] = query(ents, 3)
    k[0] = nn(x[0], w[4]).astype(BF16)
    v[0] = (nn(x[0], w[5]) + b[5:6]).astype(BF16)


def project(x, w, b):
    seqs, length, width = x.shape
    cols = 256
    out = jax.ShapeDtypeStruct((seqs, length, width), BF16)
    spec = pl.BlockSpec((1, length, cols), lambda j, s: (s, 0, j))
    return pl.pallas_call(
        project_kernel,
        grid=(width // cols, seqs),
        in_specs=[
            pl.BlockSpec((1, length, width), lambda j, s: (s, 0, 0)),
            pl.BlockSpec((6, width, cols), lambda j, s: (0, 0, j)),
            pl.BlockSpec((16, cols), lambda j, s: (0, j)),
        ],
        out_specs=[spec] * 4,
        out_shape=[out] * 4,
        compiler_params=vmem(48),
        name="project",
    )(x, w, b)


def head_mask(h):
    lane = lax.broadcasted_iota(jnp.int32, (1, 2 * HD), 1)
    return jnp.where(lane // HD == h, 1.0, 0.0).astype(BF16)


def attend_kernel(segr, segc, qw, qe, k, v, o, lse, bias, *, step):
    @pl.when(pl.program_id(1) == 0)
    def _():
        bias[...] = jnp.where(segc[0] == segr[0], 0.0, MASKED)

    length = k.shape[1]
    kp = k[0]
    vt = v[0].T
    for s, n in spans(length, step):
        parts = []
        for h in range(2):
            kh = kp * head_mask(h)
            st = jnp.concatenate(
                [nt(kh[:WORDS], qw[0, s:s + n]), nt(kh[WORDS:], qe[0, s:s + n])], axis=0
            ) + bias[:, s:s + n]
            peak = jnp.max(st, axis=0, keepdims=True)
            pt = jnp.exp(st - peak)
            total = jnp.sum(pt, axis=0, keepdims=True)
            ot = nn(vt[h * HD:(h + 1) * HD], pt.astype(BF16))
            parts.append(ot * (1.0 / total))
            lse[0, 0, h:h + 1, s:s + n] = peak + jnp.log(total)
        o[0, s:s + n] = jnp.concatenate(parts, axis=0).T.astype(BF16)


def attend(qw, qe, k, v, seg, step=256):
    seqs, length, width = k.shape
    pairs = width // (2 * HD)
    spec = pl.BlockSpec((1, length, 2 * HD), lambda s, h: (s, 0, h))
    return pl.pallas_call(
        functools.partial(attend_kernel, step=step),
        grid=(seqs, pairs),
        in_specs=[
            pl.BlockSpec((1, 1, length), lambda s, h: (s, 0, 0)),
            pl.BlockSpec((1, length, 1), lambda s, h: (s, 0, 0)),
            spec, spec, spec, spec,
        ],
        out_specs=[spec, pl.BlockSpec((1, 1, 2, length), lambda s, h: (s, h, 0, 0))],
        out_shape=[
            jax.ShapeDtypeStruct((seqs, length, width), BF16),
            jax.ShapeDtypeStruct((seqs, pairs, 2, length), F32),
        ],
        scratch_shapes=[pltpu.VMEM((length, length), F32)],
        compiler_params=vmem(48),
        name="attend",
    )(seg[:, None, :], seg[:, :, None], qw, qe, k, v)


def attend_back_kernel(segr, segc, qw, qe, k, v, o, g, lse, dqw, dqe, dk, dv, bias, *, step):
    @pl.when(pl.program_id(1) == 0)
    def _():
        bias[...] = jnp.where(segc[0] == segr[0], 0.0, MASKED)

    length = k.shape[1]
    kp = k[0]
    kt = kp.T
    vp = v[0]
    scale = HD ** -0.5
    dv_sum = None
    for i, (s, n) in enumerate(spans(length, step)):
        qws = qw[0, s:s + n]
        qes = qe[0, s:s + n]
        gs = g[0, s:s + n]
        prod = (gs.astype(F32) * o[0, s:s + n].astype(F32)).T
        dqw_parts = []
        dqe_parts = []
        for h in range(2):
            m = head_mask(h)
            kh = kp * m
            delta = jnp.sum(prod[h * HD:(h + 1) * HD], axis=0, keepdims=True)
            st = jnp.concatenate([nt(kh[:WORDS], qws), nt(kh[WORDS:], qes)], axis=0)
            pt = jnp.exp(st + bias[:, s:s + n] - lse[0, 0, h:h + 1, s:s + n])
            dpt = nt(vp * m, gs)
            dst = (pt * (dpt - delta)).astype(BF16)
            gv = nn(pt.astype(BF16), gs * m)
            gk_w = nn(dst[:WORDS], qws * m)
            gk_e = nn(dst[WORDS:], qes * m)
            kth = kt[h * HD:(h + 1) * HD]
            dqw_parts.append(nn(kth[:, :WORDS], dst[:WORDS]))
            dqe_parts.append(nn(kth[:, WORDS:], dst[WORDS:]))
            if h == 0:
                gv_p, gkw_p, gke_p = gv, gk_w, gk_e
            else:
                gv_p, gkw_p, gke_p = gv_p + gv, gkw_p + gk_w, gke_p + gk_e
        dqw[0, s:s + n] = (jnp.concatenate(dqw_parts, axis=0).T * scale).astype(BF16)
        dqe[0, s:s + n] = (jnp.concatenate(dqe_parts, axis=0).T * scale).astype(BF16)
        if i == 0:
            dv_sum, dkw_sum, dke_sum = gv_p, gkw_p, gke_p
        else:
            dv_sum, dkw_sum, dke_sum = dv_sum + gv_p, dkw_sum + gkw_p, dke_sum + gke_p
    dv[0] = dv_sum.astype(BF16)
    dk[0, :WORDS] = dkw_sum.astype(BF16)
    dk[0, WORDS:] = dke_sum.astype(BF16)


def attend_back(qw, qe, k, v, seg, o, g, lse, step=256):
    seqs, length, width = k.shape
    pairs = width // (2 * HD)
    spec = pl.BlockSpec((1, length, 2 * HD), lambda s, h: (s, 0, h))
    out = jax.ShapeDtypeStruct((seqs, length, width), BF16)
    return pl.pallas_call(
        functools.partial(attend_back_kernel, step=step),
        grid=(seqs, pairs),
        in_specs=[
            pl.BlockSpec((1, 1, length), lambda s, h: (s, 0, 0)),
            pl.BlockSpec((1, length, 1), lambda s, h: (s, 0, 0)),
            spec, spec, spec, spec, spec, spec,
            pl.BlockSpec((1, 1, 2, length), lambda s, h: (s, h, 0, 0)),
        ],
        out_specs=[spec] * 4,
        out_shape=[out] * 4,
        scratch_shapes=[pltpu.VMEM((length, length), F32)],
        compiler_params=vmem(48),
        name="attend_back",
    )(seg[:, None, :], seg[:, :, None], qw, qe, k, v, o, g, lse)


def norm_forward(values):
    center = values - jnp.mean(values, axis=-1, keepdims=True)
    scale = lax.rsqrt(jnp.mean(center * center, axis=-1, keepdims=True) + norm_eps)
    return center * scale, scale


def norm_backward(grad, normed, scale):
    first = jnp.mean(grad, axis=-1, keepdims=True)
    second = jnp.mean(grad * normed, axis=-1, keepdims=True)
    return scale * (grad - first - normed * second)


def gelu_pair(u):
    z = jnp.abs(u) * (0.5 ** 0.5)
    t = 1.0 / (1.0 + 0.3275911 * z)
    e = jnp.exp(u * u * -0.5)
    poly = 0.5 * 1.061405429
    poly = poly * t + 0.5 * -1.453152027
    poly = poly * t + 0.5 * 1.421413741
    poly = poly * t + 0.5 * -0.284496736
    poly = poly * t + 0.5 * 0.254829592
    tail = poly * t * e
    cdf = jnp.where(u < 0, tail, 1.0 - tail)
    return cdf, cdf + u * (e * 0.3989422804014327)


def colsum(v):
    return jnp.sum(v, axis=0, keepdims=True)


OUT_BIAS, GAIN_ATTN, SHIFT_ATTN, DOWN_BIAS, GAIN_FFN, SHIFT_FFN = range(6)


def middle_kernel(x, ctx, cot, wo, wi, wd, small, ib, out, gpre, hl, act, gu, gfed, gatt, gctx,
                  sums, ibsum, slope, *, step):
    @pl.when(pl.program_id(0) == 0)
    def _():
        sums[...] = jnp.zeros_like(sums)
        ibsum[...] = jnp.zeros_like(ibsum)

    def row(i):
        return small[i:i + 1]

    ff = wi.shape[1]
    attended = nn(ctx[...], wo[...]) + row(OUT_BIAS)
    normed_attn, scale_attn = norm_forward(x[...].astype(F32) + attended)
    hidden = normed_attn * row(GAIN_ATTN) + row(SHIFT_ATTN)
    low = hidden.astype(BF16)
    hl[...] = low
    fed = jnp.broadcast_to(row(DOWN_BIAS), hidden.shape)
    for s, n in spans(ff, step):
        u = nn(low, wi[:, s:s + n]) + ib[:, s:s + n]
        cdf, grad = gelu_pair(u)
        slope[:, s:s + n] = grad
        a = (u * cdf).astype(BF16)
        act[:, s:s + n] = a
        fed = fed + nn(a, wd[s:s + n])
    normed_ffn, scale_ffn = norm_forward(hidden + fed)
    out[...] = (normed_ffn * row(GAIN_FFN) + row(SHIFT_FFN)).astype(BF16)
    gy = cot[...].astype(F32)
    sums[GAIN_FFN:GAIN_FFN + 1] += colsum(gy * normed_ffn)
    sums[SHIFT_FFN:SHIFT_FFN + 1] += colsum(gy)
    gsum = norm_backward(gy * row(GAIN_FFN), normed_ffn, scale_ffn)
    gf = gsum.astype(BF16)
    gfed[...] = gf
    sums[DOWN_BIAS:DOWN_BIAS + 1] += colsum(gf.astype(F32))
    ghid = gsum
    for s, n in spans(ff, step):
        d = nt(gf, wd[s:s + n]) * slope[:, s:s + n]
        ibsum[:, s:s + n] += colsum(d)
        d = d.astype(BF16)
        gu[:, s:s + n] = d
        ghid = ghid + nt(d, wi[:, s:s + n])
    sums[GAIN_ATTN:GAIN_ATTN + 1] += colsum(ghid * normed_attn)
    sums[SHIFT_ATTN:SHIFT_ATTN + 1] += colsum(ghid)
    gp = norm_backward(ghid * row(GAIN_ATTN), normed_attn, scale_attn)
    gpre[...] = gp
    ga = gp.astype(BF16)
    gatt[...] = ga
    sums[OUT_BIAS:OUT_BIAS + 1] += colsum(ga.astype(F32))
    gctx[...] = nt(ga, wo[...]).astype(BF16)


def middle(x, ctx, cot, wo, wi, wd, small, ib, rows=256, step=512):
    total, width = x.shape
    ff = wi.shape[1]

    def block(n):
        return pl.BlockSpec((rows, n), lambda i: (i, 0))

    def whole(*shape):
        return pl.BlockSpec(shape, lambda i: (0, 0), pipeline_mode=pl.Buffered(1))

    def out(n, dtype):
        return jax.ShapeDtypeStruct((total, n), dtype)

    return pl.pallas_call(
        functools.partial(middle_kernel, step=step),
        grid=(total // rows,),
        in_specs=[
            block(width), block(width), block(width),
            whole(width, width), whole(width, ff), whole(ff, width),
            whole(8, width), whole(1, ff),
        ],
        out_specs=[
            block(width), block(width), block(width), block(ff), block(ff),
            block(width), block(width), block(width),
            pl.BlockSpec((8, width), lambda i: (0, 0)),
            pl.BlockSpec((1, ff), lambda i: (0, 0)),
        ],
        out_shape=[
            out(width, BF16), out(width, F32), out(width, BF16), out(ff, BF16), out(ff, BF16),
            out(width, BF16), out(width, BF16), out(width, BF16),
            jax.ShapeDtypeStruct((8, width), F32),
            jax.ShapeDtypeStruct((1, ff), F32),
        ],
        scratch_shapes=[pltpu.VMEM((rows, ff), F32)],
        compiler_params=vmem(60),
        name="middle",
    )(x, ctx, cot, wo, wi, wd, small, ib)


def ffn_grads_kernel(hl, gu, act_lo, act_hi, gfed, ctx, gatt, dwi, dwd, dwo, hlt):
    @pl.when(pl.program_id(0) == 0)
    def _():
        hlt[...] = hl[...].T
        dwo[0] = nn(ctx[...].T, gatt[...]).astype(BF16)

    half = act_lo.shape[1]
    dwi[0] = nn(hlt[...], gu[...]).astype(BF16)
    dwd[0, :half] = nn(act_lo[...].T, gfed[...]).astype(BF16)
    dwd[0, half:] = nn(act_hi[...].T, gfed[...]).astype(BF16)


def ffn_grads(hl, gu, act, gfed, ctx, gatt):
    total, width = hl.shape
    count = gu.shape[1] // width
    half = width // 2

    def whole():
        return pl.BlockSpec((total, width), lambda j: (0, 0), pipeline_mode=pl.Buffered(1))

    square = pl.BlockSpec((1, width, width), lambda j: (j, 0, 0))
    return pl.pallas_call(
        ffn_grads_kernel,
        grid=(count,),
        in_specs=[
            whole(),
            pl.BlockSpec((total, width), lambda j: (0, j)),
            pl.BlockSpec((total, half), lambda j: (0, j)),
            pl.BlockSpec((total, half), lambda j: (0, count + j)),
            whole(), whole(), whole(),
        ],
        out_specs=[square, square, pl.BlockSpec((1, width, width), lambda j: (0, 0, 0))],
        out_shape=[
            jax.ShapeDtypeStruct((count, width, width), BF16),
            jax.ShapeDtypeStruct((count, width, width), BF16),
            jax.ShapeDtypeStruct((1, width, width), BF16),
        ],
        scratch_shapes=[pltpu.VMEM((width, total), BF16)],
        compiler_params=vmem(60),
        name="ffn_grads",
    )(hl, gu, act, act, gfed, ctx, gatt)


def input_grads_kernel(dqw, dqe, dk, dv, w, gpre, dx):
    dx[0, :WORDS] = (
        gpre[0, :WORDS] + nt(dqw[0, :WORDS], w[0]) + nt(dqe[0, :WORDS], w[1])
        + nt(dk[0, :WORDS], w[4]) + nt(dv[0, :WORDS], w[5])
    )
    dx[0, WORDS:] = (
        gpre[0, WORDS:] + nt(dqw[0, WORDS:], w[2]) + nt(dqe[0, WORDS:], w[3])
        + nt(dk[0, WORDS:], w[4]) + nt(dv[0, WORDS:], w[5])
    )


def input_grads(dqw, dqe, dk, dv, w, gpre):
    seqs, length, width = dqw.shape
    cols = 256
    full = pl.BlockSpec((1, length, width), lambda j, s: (s, 0, 0))
    part = pl.BlockSpec((1, length, cols), lambda j, s: (s, 0, j))
    return pl.pallas_call(
        input_grads_kernel,
        grid=(width // cols, seqs),
        in_specs=[full] * 4 + [pl.BlockSpec((6, cols, width), lambda j, s: (0, j, 0)), part],
        out_specs=part,
        out_shape=jax.ShapeDtypeStruct((seqs, length, width), F32),
        compiler_params=vmem(48),
        name="input_grads",
    )(dqw, dqe, dk, dv, w, gpre)


def qkv_grads_kernel(x, dqw, dqe, dk, dv, dw, sums, xt):
    seqs, length, width = x.shape

    @pl.when(pl.program_id(0) == 0)
    def _():
        for s in range(seqs):
            xt[s] = x[s].T

    def grad(source, lo, hi):
        total = nn(xt[0, :, lo:hi], source[0, lo:hi])
        for s in range(1, seqs):
            total = total + nn(xt[s, :, lo:hi], source[s, lo:hi])
        return total.astype(BF16)

    def bias(source, lo, hi):
        total = colsum(source[0, lo:hi].astype(F32))
        for s in range(1, seqs):
            total = total + colsum(source[s, lo:hi].astype(F32))
        return total

    for i, (source, lo, hi) in enumerate([
        (dqw, 0, WORDS), (dqe, 0, WORDS), (dqw, WORDS, length), (dqe, WORDS, length),
        (dk, 0, length), (dv, 0, length),
    ]):
        dw[i] = grad(source, lo, hi)
        if i != 4:
            sums[i:i + 1] = bias(source, lo, hi)


def qkv_grads(x, dqw, dqe, dk, dv, cols=256):
    seqs, length, width = x.shape
    part = pl.BlockSpec((seqs, length, cols), lambda j: (0, 0, j))
    return pl.pallas_call(
        qkv_grads_kernel,
        grid=(width // cols,),
        in_specs=[pl.BlockSpec((seqs, length, width), lambda j: (0, 0, 0), pipeline_mode=pl.Buffered(1))]
        + [part] * 4,
        out_specs=[
            pl.BlockSpec((6, width, cols), lambda j: (0, 0, j)),
            pl.BlockSpec((8, cols), lambda j: (0, j)),
        ],
        out_shape=[
            jax.ShapeDtypeStruct((6, width, width), BF16),
            jax.ShapeDtypeStruct((8, width), F32),
        ],
        scratch_shapes=[pltpu.VMEM((seqs, width, length), BF16)],
        compiler_params=vmem(60),
        name="qkv_grads",
    )(x, dqw, dqe, dk, dv)

MESH = pl.DeviceIdType.MESH
UNIT = 384


def place():
    d = lax.axis_index("dp")
    f = lax.axis_index("fsdp")
    bits = {"core": d % 2, "y": (d // 2) % 2, "z0": (d // 4) % 2, "z1": (d // 8) % 2, "x": f}
    peers = {"x": {"fsdp": 1 - f}}
    for name, size in (("core", 1), ("y", 2), ("z0", 4), ("z1", 8)):
        peers[name] = {"dp": d + size - 2 * size * bits[name]}
    return bits, peers


def greet(peers, names):
    barrier = pltpu.get_barrier_semaphore()
    for name in names:
        pl.semaphore_signal(barrier, inc=1, device_id=peers[name], device_id_type=MESH)
    pl.semaphore_wait(barrier, len(names))


def gather_kernel(*refs, units):
    n_own = 1 + max(u[0] for u in units)
    own = refs[:n_own]
    small = refs[n_own]
    w6, wo, wi, wd, table = refs[n_own + 1:n_own + 6]
    held, small_held, send, recv, local, small_sem = refs[n_own + 6:]
    bits, peers = place()
    greet(peers, ("x", "y", "z0", "core"))
    f, c = bits["x"], bits["core"]
    piece = UNIT // 8

    def src(u, rows, size):
        i, kind, k = units[u]
        if kind == "wi":
            return own[i].at[pl.ds(rows, size), k * 768:(k + 1) * 768]
        return own[i].at[pl.ds(k * UNIT + rows, size)]

    def dst(u, half, rows, size):
        i, kind, k = units[u]
        if kind == "w6":
            return w6.at[i, pl.ds(half * UNIT + rows, size)]
        if kind == "wo":
            return wo.at[pl.ds(half * UNIT + rows, size)]
        if kind == "wi":
            return wi.at[pl.ds(half * UNIT + rows, size), k * 768:(k + 1) * 768]
        return wd.at[pl.ds(half * 4 * UNIT + k * UNIT + rows, size)]

    def remote(u, stage, a, b, peer):
        return pltpu.make_async_remote_copy(
            src_ref=a, dst_ref=b, send_sem=send.at[u, stage], recv_sem=recv.at[u, stage],
            device_id=peers[peer], device_id_type=MESH,
        )

    def order(u):
        return ("y", "z0") if u % 2 == 0 else ("z0", "y")

    def copy(u, stage):
        first, second = order(u)
        a, b = bits[first], bits[second]
        mine = (c * 4 + b * 2 + a) * piece
        pair = (c * 4 + b * 2) * piece
        away = (c * 4 + (1 - b) * 2) * piece
        if stage == 0:
            return remote(u, 0, src(u, mine, piece), dst(u, f, mine, piece), "x")
        if stage == 1:
            here = dst(u, 1 - f, mine, piece)
            return remote(u, 1, here, here, first)
        if stage == 2:
            here = dst(u, 1 - f, pair, 2 * piece)
            return remote(u, 2, here, here, second)
        here = dst(u, 1 - f, pair if stage == 3 else away, 2 * piece)
        return remote(u, stage, here, here, "core")

    n = len(units)
    for u in range(n):
        copy(u, 0).start()
    small_copy = pltpu.make_async_remote_copy(
        src_ref=small, dst_ref=table.at[f], send_sem=small_sem.at[0], recv_sem=small_sem.at[1],
        device_id=peers["x"], device_id_type=MESH,
    )
    small_copy.start()

    def load(u):
        return pltpu.make_async_copy(src(u, 0, UNIT), held.at[u], local.at[u])

    def store(u):
        return pltpu.make_async_copy(held.at[u], dst(u, f, 0, UNIT), local.at[u])

    for u in range(n):
        load(u).start()
    small_in = pltpu.make_async_copy(small, small_held, small_sem.at[2])
    small_in.start()
    small_in.wait()
    small_out = pltpu.make_async_copy(small_held, table.at[f], small_sem.at[2])
    small_out.start()
    for t in range(n + 2):
        if t < n:
            copy(t, 0).wait_recv()
            copy(t, 1).start()
            load(t).wait()
            store(t).start()
        if 0 <= t - 1 < n:
            copy(t - 1, 1).wait_recv()
            copy(t - 1, 2).start()
            copy(t - 1, 3).start()
        if 0 <= t - 2 < n:
            copy(t - 2, 2).wait_recv()
            copy(t - 2, 4).start()
    for u in range(n):
        copy(u, 3).wait_recv()
        copy(u, 4).wait_recv()
        for stage in range(5):
            copy(u, stage).wait_send()
        store(u).wait()
    small_copy.wait()
    small_out.wait()


def gather(own, small):
    units = [(i, "w6", 0) for i in range(6)] + [(6, "wo", 0)]
    units += [(7, "wi", k) for k in range(4)] + [(8, "wd", k) for k in range(4)]
    n = len(units)
    any_spec = pl.BlockSpec(memory_space=pl.ANY)
    width = own[0].shape[1]
    ff = own[7].shape[1]
    return pl.pallas_call(
        functools.partial(gather_kernel, units=units),
        in_specs=[any_spec] * 10,
        out_specs=[any_spec] * 5,
        out_shape=[
            jax.ShapeDtypeStruct((6, width, width), BF16),
            jax.ShapeDtypeStruct((width, width), BF16),
            jax.ShapeDtypeStruct((width, ff), BF16),
            jax.ShapeDtypeStruct((ff, width), BF16),
            jax.ShapeDtypeStruct((2,) + small.shape, small.dtype),
        ],
        scratch_shapes=[
            pltpu.VMEM((n, UNIT, width), BF16),
            pltpu.VMEM(small.shape, small.dtype),
            pltpu.SemaphoreType.DMA((n, 5)),
            pltpu.SemaphoreType.DMA((n, 5)),
            pltpu.SemaphoreType.DMA((n,)),
            pltpu.SemaphoreType.DMA((3,)),
        ],
        compiler_params=pltpu.CompilerParams(
            collective_id=0, has_side_effects=True, vmem_limit_bytes=48 * 1024 * 1024
        ),
        name="gather_params",
    )(*own, small)


STAGES = ("core", "x", "y", "z0", "z1")
BACK = ("z1", "z0", "y", "core")


def reduce_kernel(*refs, counts, has_small):
    n_in = len(counts)
    grads = refs[:n_in]
    if has_small:
        small_in, out, small_out = refs[n_in:n_in + 3]
        rest = refs[n_in + 3:]
    else:
        out = refs[n_in]
        rest = refs[n_in + 1:]
    own, from_core, from_x, from_y, from_z0, from_z1, full, send, recv, local = rest[:10]
    if has_small:
        small_sum, small_got, small_send, small_recv = rest[10:]
    bits, peers = place()
    greet(peers, STAGES)
    half = UNIT
    c, f = bits["core"], bits["x"]
    total = sum(counts)
    mine = pl.multiple_of(c * half, half)
    theirs = pl.multiple_of((1 - c) * half, half)

    def remote(u, stage, a, b, peer):
        return pltpu.make_async_remote_copy(
            src_ref=a, dst_ref=b, send_sem=send.at[u, stage], recv_sem=recv.at[u, stage],
            device_id=peers[peer], device_id_type=MESH,
        )

    y0 = bits["y"] * 192
    z00 = y0 + bits["z0"] * 96
    z10 = z00 + bits["z1"] * 48
    y1 = (1 - bits["y"]) * 192
    z01 = y0 + (1 - bits["z0"]) * 96
    z11 = z00 + (1 - bits["z1"]) * 48

    def rows(start, size):
        return pl.ds(pl.multiple_of(start, 16), size)

    def first(g, k, u):
        return remote(u, 0, g.at[k, :, pl.ds(theirs, half)], from_core.at[u], "core")

    def load(g, k, u):
        return pltpu.make_async_copy(g.at[k, :, pl.ds(mine, half)], own.at[u], local.at[u])

    def copy(u, stage):
        if stage == 1:
            return remote(u, 1, own.at[u, rows((1 - f) * UNIT, UNIT)], from_x.at[u], "x")
        if stage == 2:
            return remote(u, 2, own.at[u, rows(f * UNIT + y1, 192)], from_y.at[u], "y")
        if stage == 3:
            return remote(u, 3, own.at[u, rows(f * UNIT + z01, 96)], from_z0.at[u], "z0")
        if stage == 4:
            return remote(u, 4, own.at[u, rows(f * UNIT + z11, 48)], from_z1.at[u], "z1")
        start, size, peer = {5: (z10, 48, "z1"), 6: (z00, 96, "z0"), 7: (y0, 192, "y"), 8: (0, 384, "core")}[stage]
        here = full.at[u, rows(start, size), pl.ds(mine, half)]
        return remote(u, stage, here, here, peer)

    def add(u, start, size, got):
        here = rows(start, size)
        own[u, here] = (own[u, here].astype(F32) + got.astype(F32)).astype(BF16)

    base = 0
    for g, count in zip(grads, counts):
        def begin(k, carry, g=g, base=base):
            first(g, k, base + k).start()
            load(g, k, base + k).start()
            return carry
        lax.fori_loop(0, count, begin, 0)
        base += count

    def small_copy(s):
        return pltpu.make_async_remote_copy(
            src_ref=small_sum.at[s], dst_ref=small_got.at[s], send_sem=small_send.at[s],
            recv_sem=small_recv.at[s], device_id=peers[STAGES[s]], device_id_type=MESH,
        )

    if has_small:
        small_sum[0] = small_in[...]
        small_copy(0).start()

    def out_copy(u):
        return pltpu.make_async_copy(full.at[u], out.at[u], local.at[u])

    def step(t, carry):
        @pl.when(t < total)
        def _():
            u = t
            first(grads[0], 0, u).wait_recv()
            load(grads[0], 0, u).wait()
            for k in range(2):
                add(u, k * UNIT, UNIT, from_core[u, k * UNIT:(k + 1) * UNIT])
            copy(u, 1).start()

        def at(lag, body):
            @pl.when(jnp.logical_and(t >= lag, t < total + lag))
            def _():
                body(t - lag)

        def after_x(u):
            copy(u, 1).wait_recv()
            add(u, f * UNIT, UNIT, from_x[u])
            copy(u, 2).start()

        def after_y(u):
            copy(u, 2).wait_recv()
            add(u, f * UNIT + y0, 192, from_y[u])
            copy(u, 3).start()

        def after_z0(u):
            copy(u, 3).wait_recv()
            add(u, f * UNIT + z00, 96, from_z0[u])
            copy(u, 4).start()

        def after_z1(u):
            copy(u, 4).wait_recv()
            here = rows(f * UNIT + z10, 48)
            full[u, rows(z10, 48), pl.ds(mine, half)] = (
                own[u, here].astype(F32) + from_z1[u].astype(F32)
            ).astype(BF16)
            copy(u, 5).start()

        def forward(stage):
            def body(u):
                copy(u, stage).wait_recv()
                copy(u, stage + 1).start()
            return body

        def finish(u):
            copy(u, 8).wait_recv()
            out_copy(u).start()

        at(2, after_x)
        at(3, after_y)
        at(4, after_z0)
        at(5, after_z1)
        at(6, forward(5))
        at(7, forward(6))
        at(8, forward(7))
        at(9, finish)

        if has_small:
            for s in range(5):
                @pl.when(t == 1 + s)
                def _(s=s):
                    small_copy(s).wait_recv()
                    value = small_sum[s] + small_got[s]
                    if s < 4:
                        small_sum[s + 1] = value
                        small_copy(s + 1).start()
                    else:
                        small_out[...] = value
        return carry

    lax.fori_loop(0, total + 9, step, 0)

    def drain(u, carry):
        first(grads[0], 0, u).wait_send()
        for stage in range(1, 9):
            copy(u, stage).wait_send()
        out_copy(u).wait()
        return carry

    lax.fori_loop(0, total, drain, 0)
    if has_small:
        for s in range(5):
            small_copy(s).wait_send()


def reduce_grads(grads, small=None, collective_id=1):
    counts = [g.shape[0] for g in grads]
    total = sum(counts)
    width = grads[0].shape[2]
    any_spec = pl.BlockSpec(memory_space=pl.ANY)
    vm = pl.BlockSpec(memory_space=pltpu.VMEM)
    has_small = small is not None
    scratch = [
        pltpu.VMEM((total, 2 * UNIT, UNIT), BF16),
        pltpu.VMEM((total, 2 * UNIT, UNIT), BF16),
        pltpu.VMEM((total, 384, UNIT), BF16),
        pltpu.VMEM((total, 192, UNIT), BF16),
        pltpu.VMEM((total, 96, UNIT), BF16),
        pltpu.VMEM((total, 48, UNIT), BF16),
        pltpu.VMEM((total, 384, 2 * UNIT), BF16),
        pltpu.SemaphoreType.DMA((total, 9)),
        pltpu.SemaphoreType.DMA((total, 9)),
        pltpu.SemaphoreType.DMA((total,)),
    ]
    out_shape = [jax.ShapeDtypeStruct((total, UNIT, width), BF16)]
    if has_small:
        scratch += [
            pltpu.VMEM((5,) + small.shape, F32),
            pltpu.VMEM((5,) + small.shape, F32),
            pltpu.SemaphoreType.DMA((5,)),
            pltpu.SemaphoreType.DMA((5,)),
        ]
        out_shape.append(jax.ShapeDtypeStruct(small.shape, F32))
    res = pl.pallas_call(
        functools.partial(reduce_kernel, counts=counts, has_small=has_small),
        in_specs=[any_spec] * len(grads) + [vm] * has_small,
        out_specs=[any_spec] + [vm] * has_small,
        out_shape=out_shape,
        scratch_shapes=scratch,
        compiler_params=pltpu.CompilerParams(
            collective_id=collective_id, has_side_effects=True, vmem_limit_bytes=60 * 1024 * 1024
        ),
        name="reduce_grads",
    )(*grads, *([small] if has_small else []))
    return res if has_small else res[0]


def local(
    inputs, segments,
    query_wordword, query_wordent, query_entword, query_entent,
    bias_wordword, bias_wordent, bias_entword, bias_entent,
    key_weight, value_weight, value_bias, out_weight, out_bias,
    gain_attn, shift_attn, inner_weight, inner_bias, down_weight, down_bias,
    gain_ffn, shift_ffn, cotangent, *, dp, fsdp,
):
    seqs, length, width = inputs.shape
    share = width // fsdp
    ff = inner_weight.shape[1]
    paired = dp == 16 and fsdp == 2

    def gather_all(value):
        return lax.all_gather(value, "fsdp", axis=0, tiled=True)

    zero = jnp.zeros((share,), BF16)
    packed = jnp.concatenate([
        jnp.stack([
            bias_wordword, bias_wordent, bias_entword, bias_entent, zero, value_bias,
            out_bias, gain_attn, shift_attn, down_bias, gain_ffn, shift_ffn,
        ]),
        inner_bias.reshape(4, share),
    ])
    own = (query_wordword, query_wordent, query_entword, query_entent, key_weight, value_weight,
           out_weight, inner_weight, down_weight)
    if paired:
        w6, wo, wi, wd, table = gather(own, packed)
    else:
        w6 = jnp.stack([gather_all(w) for w in own[:6]])
        wo, wi, wd = [gather_all(w) for w in own[6:]]
        table = lax.all_gather(packed, "fsdp", axis=0)
    wide = table.transpose(1, 0, 2).reshape(16, width).astype(F32)
    ib = table[:, 12:].reshape(1, ff).astype(F32)

    qw, qe, keys, vals = project(inputs, w6, wide)
    ctx, lse = attend(qw, qe, keys, vals, segments)

    def flat(value):
        return value.reshape(seqs * length, width)

    ctx_rows = flat(ctx)
    out, gpre, hl, act, gu, gfed, gatt, gctx, sums, ibsum = middle(
        flat(inputs), ctx_rows, flat(cotangent), wo, wi, wd, wide[6:14], ib)
    units = ffn_grads(hl, gu, act, gfed, ctx_rows, gatt)
    dqw, dqe, dk, dv = attend_back(
        qw, qe, keys, vals, segments, ctx, gctx.reshape(inputs.shape), lse)
    grad_inputs = input_grads(dqw, dqe, dk, dv, w6, gpre.reshape(inputs.shape))
    dw6, qsums = qkv_grads(inputs, dqw, dqe, dk, dv)
    small = jnp.concatenate([sums, qsums, ibsum.reshape(4, width), jnp.zeros((4, width), F32)])
    f = lax.axis_index("fsdp")

    if paired:
        grads, totals = reduce_grads([*units, dw6], small)
        grads = grads.astype(F32)
        g_wi = grads[:4].transpose(1, 0, 2).reshape(share, ff)
        g_wd = grads[4:8].reshape(4 * share, width)
        g_wo = grads[8]
        g6 = [grads[9 + i] for i in range(6)]
    else:
        def shared(grad):
            part = lax.psum_scatter(grad, "fsdp", scatter_dimension=0, tiled=True)
            return lax.psum(part, "dp").astype(F32)

        g_wi = shared(units[0].transpose(1, 0, 2).reshape(width, ff))
        g_wd = shared(units[1].reshape(4, 2, width // 2, width).transpose(1, 0, 2, 3).reshape(ff, width))
        g_wo = shared(units[2][0])
        g6 = [shared(dw6[i]) for i in range(6)]
        totals = lax.psum(small, ("dp", "fsdp"))

    mine = lax.dynamic_slice_in_dim(totals[:16], f * share, share, axis=1)
    g_ib = lax.dynamic_slice_in_dim(totals[16:20].reshape(ff), f * (ff // fsdp), ff // fsdp)
    return (
        out.reshape(inputs.shape), grad_inputs,
        g6[0], g6[1], g6[2], g6[3],
        mine[8], mine[9], mine[10], mine[11],
        g6[4], g6[5], mine[13],
        g_wo, mine[OUT_BIAS], mine[GAIN_ATTN], mine[SHIFT_ATTN],
        g_wi, g_ib, g_wd, mine[DOWN_BIAS], mine[GAIN_FFN], mine[SHIFT_FFN],
    )


def solution(mesh):
    rows = P(("dp", "fsdp"), None, None)
    mat = P("fsdp", None)
    vec = P("fsdp")
    params = (mat,) * 4 + (vec,) * 4 + (mat, mat, vec, mat, vec, vec, vec, mat, vec, mat, vec, vec, vec)
    return jax.shard_map(
        functools.partial(local, dp=mesh.shape["dp"], fsdp=mesh.shape["fsdp"]),
        mesh=mesh,
        in_specs=(rows, P(("dp", "fsdp"), None)) + params + (rows,),
        out_specs=(rows, rows) + params,
        check_vma=False,
    )
```

```python
import functools
import jax
import jax.numpy as jnp
from jax import lax
from jax.experimental import pallas as pl
from jax.experimental.pallas import tpu as pltpu
from jax.sharding import PartitionSpec as P

HD = 64
WORDS = 512
norm_eps = 1e-12
F32 = jnp.float32
BF16 = jnp.bfloat16
MASKED = -1000000000.0


def nn(a, b):
    return lax.dot_general(a, b, (((1,), (0,)), ((), ())), preferred_element_type=F32)


def nt(a, b):
    return lax.dot_general(a, b, (((1,), (1,)), ((), ())), preferred_element_type=F32)


def vmem(mb):
    return pltpu.CompilerParams(vmem_limit_bytes=mb * 1024 * 1024)


def spans(total, size):
    return [(s, min(size, total - s)) for s in range(0, total, size)]


def project_kernel(x, w, b, qw, qe, k, v):
    words = x[0, :WORDS]
    ents = x[0, WORDS:]
    scale = HD ** -0.5

    def query(rows, i):
        return ((nn(rows, w[i]) + b[i:i + 1]).astype(BF16) * scale).astype(BF16)

    qw[0, :WORDS] = query(words, 0)
    qe[0, :WORDS] = query(words, 1)
    qw[0, WORDS:] = query(ents, 2)
    qe[0, WORDS:] = query(ents, 3)
    k[0] = nn(x[0], w[4]).astype(BF16)
    v[0] = (nn(x[0], w[5]) + b[5:6]).astype(BF16)


def project(x, w, b):
    seqs, length, width = x.shape
    cols = 256
    out = jax.ShapeDtypeStruct((seqs, length, width), BF16)
    spec = pl.BlockSpec((1, length, cols), lambda j, s: (s, 0, j))
    return pl.pallas_call(
        project_kernel,
        grid=(width // cols, seqs),
        in_specs=[
            pl.BlockSpec((1, length, width), lambda j, s: (s, 0, 0)),
            pl.BlockSpec((6, width, cols), lambda j, s: (0, 0, j)),
            pl.BlockSpec((16, cols), lambda j, s: (0, j)),
        ],
        out_specs=[spec] * 4,
        out_shape=[out] * 4,
        compiler_params=vmem(48),
        name="project",
    )(x, w, b)


def head_mask(h):
    lane = lax.broadcasted_iota(jnp.int32, (1, 2 * HD), 1)
    return jnp.where(lane // HD == h, 1.0, 0.0).astype(BF16)


def document_bias(seg):
    row = seg.astype(F32)
    col = jnp.broadcast_to(row, (8, row.shape[1])).T[:, :1]
    return jnp.where(col == row, 0.0, MASKED)


def attend_kernel(seg, qw, qe, k, v, o, lse, bias, *, step):
    @pl.when(pl.program_id(1) == 0)
    def _():
        bias[...] = document_bias(seg[0])

    length = k.shape[1]
    kp = k[0]
    vt = v[0].T
    for s, n in spans(length, step):
        parts = []
        for h in range(2):
            kh = kp * head_mask(h)
            st = jnp.concatenate(
                [nt(kh[:WORDS], qw[0, s:s + n]), nt(kh[WORDS:], qe[0, s:s + n])], axis=0
            ) + bias[:, s:s + n]
            peak = jnp.max(st, axis=0, keepdims=True)
            pt = jnp.exp(st - peak)
            total = jnp.sum(pt, axis=0, keepdims=True)
            ot = nn(vt[h * HD:(h + 1) * HD], pt.astype(BF16))
            parts.append(ot * (1.0 / total))
            lse[0, 0, h:h + 1, s:s + n] = peak + jnp.log(total)
        o[0, s:s + n] = jnp.concatenate(parts, axis=0).T.astype(BF16)


def attend(qw, qe, k, v, seg, step=256):
    seqs, length, width = k.shape
    pairs = width // (2 * HD)
    spec = pl.BlockSpec((1, length, 2 * HD), lambda s, h: (s, 0, h))
    return pl.pallas_call(
        functools.partial(attend_kernel, step=step),
        grid=(seqs, pairs),
        in_specs=[
            pl.BlockSpec((1, 1, length), lambda s, h: (s, 0, 0)),
            spec, spec, spec, spec,
        ],
        out_specs=[spec, pl.BlockSpec((1, 1, 2, length), lambda s, h: (s, h, 0, 0))],
        out_shape=[
            jax.ShapeDtypeStruct((seqs, length, width), BF16),
            jax.ShapeDtypeStruct((seqs, pairs, 2, length), F32),
        ],
        scratch_shapes=[pltpu.VMEM((length, length), F32)],
        compiler_params=vmem(48),
        name="attend",
    )(seg[:, None, :], qw, qe, k, v)


def attend_back_pair(qw, qe, k, v, o, g, lse, bias, put, step):
    length = k.shape[1]
    kp = k[0]
    kt = kp.T
    vp = v[0]
    scale = HD ** -0.5
    sums = None
    for s, n in spans(length, step):
        qws = qw[0, s:s + n]
        qes = qe[0, s:s + n]
        gs = g[0, s:s + n]
        prod = (gs.astype(F32) * o[0, s:s + n].astype(F32)).T
        dqw_parts = []
        dqe_parts = []
        for h in range(2):
            m = head_mask(h)
            kh = kp * m
            delta = jnp.sum(prod[h * HD:(h + 1) * HD], axis=0, keepdims=True)
            st = jnp.concatenate([nt(kh[:WORDS], qws), nt(kh[WORDS:], qes)], axis=0)
            pt = jnp.exp(st + bias[:, s:s + n] - lse[0, 0, h:h + 1, s:s + n])
            dpt = nt(vp * m, gs)
            dst = (pt * (dpt - delta)).astype(BF16)
            parts = (nn(pt.astype(BF16), gs * m), nn(dst[:WORDS], qws * m), nn(dst[WORDS:], qes * m))
            sums = parts if sums is None else tuple(a + b for a, b in zip(sums, parts))
            kth = kt[h * HD:(h + 1) * HD]
            dqw_parts.append(nn(kth[:, :WORDS], dst[:WORDS]))
            dqe_parts.append(nn(kth[:, WORDS:], dst[WORDS:]))
        put(0, s, n, (jnp.concatenate(dqw_parts, axis=0).T * scale).astype(BF16))
        put(1, s, n, (jnp.concatenate(dqe_parts, axis=0).T * scale).astype(BF16))
    put(2, 0, WORDS, sums[1].astype(BF16))
    put(2, WORDS, length - WORDS, sums[2].astype(BF16))
    put(3, 0, length, sums[0].astype(BF16))


def attend_back_kernel(seg, qw, qe, k, v, o, g, lse, dqw, dqe, dk, dv, bias, *, step):
    @pl.when(pl.program_id(1) == 0)
    def _():
        bias[...] = document_bias(seg[0])

    def put(slot, lo, n, value):
        (dqw, dqe, dk, dv)[slot][0, lo:lo + n] = value

    attend_back_pair(qw, qe, k, v, o, g, lse, bias, put, step)


def attend_back(qw, qe, k, v, seg, o, g, lse, step=256):
    seqs, length, width = k.shape
    pairs = width // (2 * HD)
    spec = pl.BlockSpec((1, length, 2 * HD), lambda s, h: (s, 0, h))
    out = jax.ShapeDtypeStruct((seqs, length, width), BF16)
    return pl.pallas_call(
        functools.partial(attend_back_kernel, step=step),
        grid=(seqs, pairs),
        in_specs=[
            pl.BlockSpec((1, 1, length), lambda s, h: (s, 0, 0)),
            spec, spec, spec, spec, spec, spec,
            pl.BlockSpec((1, 1, 2, length), lambda s, h: (s, h, 0, 0)),
        ],
        out_specs=[spec] * 4,
        out_shape=[out] * 4,
        scratch_shapes=[pltpu.VMEM((length, length), F32)],
        compiler_params=vmem(48),
        name="attend_back",
    )(seg[:, None, :], qw, qe, k, v, o, g, lse)


def norm_forward(values):
    center = values - jnp.mean(values, axis=-1, keepdims=True)
    scale = lax.rsqrt(jnp.mean(center * center, axis=-1, keepdims=True) + norm_eps)
    return center * scale, scale


def norm_backward(grad, normed, scale):
    first = jnp.mean(grad, axis=-1, keepdims=True)
    second = jnp.mean(grad * normed, axis=-1, keepdims=True)
    return scale * (grad - first - normed * second)


def gelu_pair(u):
    z = jnp.abs(u) * (0.5 ** 0.5)
    t = 1.0 / (1.0 + 0.3275911 * z)
    e = jnp.exp(u * u * -0.5)
    poly = 0.5 * 1.061405429
    poly = poly * t + 0.5 * -1.453152027
    poly = poly * t + 0.5 * 1.421413741
    poly = poly * t + 0.5 * -0.284496736
    poly = poly * t + 0.5 * 0.254829592
    tail = poly * t * e
    cdf = jnp.where(u < 0, tail, 1.0 - tail)
    return cdf, cdf + u * (e * 0.3989422804014327)


def colsum(v):
    return jnp.sum(v, axis=0, keepdims=True)


OUT_BIAS, GAIN_ATTN, SHIFT_ATTN, DOWN_BIAS, GAIN_FFN, SHIFT_FFN = range(6)


def middle_kernel(x, ctx, cot, wo, wi, wd, small, ib, out, gpre, hl, act, gu, gfed, gatt, gctx,
                  sums, slope, *, step):
    @pl.when(pl.program_id(0) == 0)
    def _():
        sums[...] = jnp.zeros_like(sums)

    def row(i):
        return small[6 + i:7 + i]

    ff = wi.shape[1]
    attended = nn(ctx[...], wo[...]) + row(OUT_BIAS)
    normed_attn, scale_attn = norm_forward(x[...].astype(F32) + attended)
    hidden = normed_attn * row(GAIN_ATTN) + row(SHIFT_ATTN)
    low = hidden.astype(BF16)
    hl[...] = low
    fed = jnp.broadcast_to(row(DOWN_BIAS), hidden.shape)
    for s, n in spans(ff, step):
        u = nn(low, wi[:, s:s + n]) + ib[:, s:s + n]
        cdf, grad = gelu_pair(u)
        slope[:, s:s + n] = grad
        a = (u * cdf).astype(BF16)
        act[:, s:s + n] = a
        fed = fed + nn(a, wd[s:s + n])
    normed_ffn, scale_ffn = norm_forward(hidden + fed)
    out[...] = (normed_ffn * row(GAIN_FFN) + row(SHIFT_FFN)).astype(BF16)
    gy = cot[...].astype(F32)
    sums[GAIN_FFN:GAIN_FFN + 1] += colsum(gy * normed_ffn)
    sums[SHIFT_FFN:SHIFT_FFN + 1] += colsum(gy)
    gsum = norm_backward(gy * row(GAIN_FFN), normed_ffn, scale_ffn)
    gf = gsum.astype(BF16)
    gfed[...] = gf
    sums[DOWN_BIAS:DOWN_BIAS + 1] += colsum(gf.astype(F32))
    ghid = gsum
    for s, n in spans(ff, step):
        d = nt(gf, wd[s:s + n]) * slope[:, s:s + n]
        sums[16 + s // n:17 + s // n] += colsum(d)
        d = d.astype(BF16)
        gu[:, s:s + n] = d
        ghid = ghid + nt(d, wi[:, s:s + n])
    sums[GAIN_ATTN:GAIN_ATTN + 1] += colsum(ghid * normed_attn)
    sums[SHIFT_ATTN:SHIFT_ATTN + 1] += colsum(ghid)
    gp = norm_backward(ghid * row(GAIN_ATTN), normed_attn, scale_attn)
    gpre[...] = gp
    ga = gp.astype(BF16)
    gatt[...] = ga
    sums[OUT_BIAS:OUT_BIAS + 1] += colsum(ga.astype(F32))
    gctx[...] = nt(ga, wo[...]).astype(BF16)


def middle(x, ctx, cot, wo, wi, wd, small, ib, rows=256, step=768):
    total, width = x.shape
    ff = wi.shape[1]

    def block(n):
        return pl.BlockSpec((rows, n), lambda i: (i, 0))

    def whole(*shape):
        return pl.BlockSpec(shape, lambda i: (0, 0), pipeline_mode=pl.Buffered(1))

    def out(n, dtype):
        return jax.ShapeDtypeStruct((total, n), dtype)

    return pl.pallas_call(
        functools.partial(middle_kernel, step=step),
        grid=(total // rows,),
        in_specs=[
            block(width), block(width), block(width),
            whole(width, width), whole(width, ff), whole(ff, width),
            whole(16, width), whole(1, ff),
        ],
        out_specs=[
            block(width), block(width), block(width), block(ff), block(ff),
            block(width), block(width), block(width),
            pl.BlockSpec((24, width), lambda i: (0, 0)),
        ],
        out_shape=[
            out(width, BF16), out(width, F32), out(width, BF16), out(ff, BF16), out(ff, BF16),
            out(width, BF16), out(width, BF16), out(width, BF16),
            jax.ShapeDtypeStruct((24, width), F32),
        ],
        scratch_shapes=[pltpu.VMEM((rows, ff), F32)],
        compiler_params=vmem(60),
        name="middle",
    )(x, ctx, cot, wo, wi, wd, small, ib)


def ffn_grads_kernel(hl, gu, act_lo, act_hi, gfed, ctx, gatt, dwi, dwd, dwo, hlt):
    @pl.when(pl.program_id(0) == 0)
    def _():
        hlt[...] = hl[...].T
        dwo[0] = nn(ctx[...].T, gatt[...]).astype(BF16)

    half = act_lo.shape[1]
    dwi[0] = nn(hlt[...], gu[...]).astype(BF16)
    dwd[0, :half] = nn(act_lo[...].T, gfed[...]).astype(BF16)
    dwd[0, half:] = nn(act_hi[...].T, gfed[...]).astype(BF16)


def ffn_grads(hl, gu, act, gfed, ctx, gatt):
    total, width = hl.shape
    count = gu.shape[1] // width
    half = width // 2

    def whole():
        return pl.BlockSpec((total, width), lambda j: (0, 0), pipeline_mode=pl.Buffered(1))

    square = pl.BlockSpec((1, width, width), lambda j: (j, 0, 0))
    return pl.pallas_call(
        ffn_grads_kernel,
        grid=(count,),
        in_specs=[
            whole(),
            pl.BlockSpec((total, width), lambda j: (0, j)),
            pl.BlockSpec((total, half), lambda j: (0, j)),
            pl.BlockSpec((total, half), lambda j: (0, count + j)),
            whole(), whole(), whole(),
        ],
        out_specs=[square, square, pl.BlockSpec((1, width, width), lambda j: (0, 0, 0))],
        out_shape=[
            jax.ShapeDtypeStruct((count, width, width), BF16),
            jax.ShapeDtypeStruct((count, width, width), BF16),
            jax.ShapeDtypeStruct((1, width, width), BF16),
        ],
        scratch_shapes=[pltpu.VMEM((width, total), BF16)],
        compiler_params=vmem(60),
        name="ffn_grads",
    )(hl, gu, act, act, gfed, ctx, gatt)


def input_grads_kernel(dqw, dqe, dk, dv, w, gpre, dx):
    dx[0, :WORDS] = (
        gpre[0, :WORDS] + nt(dqw[0, :WORDS], w[0]) + nt(dqe[0, :WORDS], w[1])
        + nt(dk[0, :WORDS], w[4]) + nt(dv[0, :WORDS], w[5])
    )
    dx[0, WORDS:] = (
        gpre[0, WORDS:] + nt(dqw[0, WORDS:], w[2]) + nt(dqe[0, WORDS:], w[3])
        + nt(dk[0, WORDS:], w[4]) + nt(dv[0, WORDS:], w[5])
    )


def input_grads(dqw, dqe, dk, dv, w, gpre):
    seqs, length, width = dqw.shape
    cols = 256
    full = pl.BlockSpec((1, length, width), lambda j, s: (s, 0, 0))
    part = pl.BlockSpec((1, length, cols), lambda j, s: (s, 0, j))
    return pl.pallas_call(
        input_grads_kernel,
        grid=(width // cols, seqs),
        in_specs=[full] * 4 + [pl.BlockSpec((6, cols, width), lambda j, s: (0, j, 0)), part],
        out_specs=part,
        out_shape=jax.ShapeDtypeStruct((seqs, length, width), F32),
        compiler_params=vmem(48),
        name="input_grads",
    )(dqw, dqe, dk, dv, w, gpre)


def qkv_grads_kernel(x, dqw, dqe, dk, dv, dw, sums, xt):
    seqs, length, width = x.shape

    @pl.when(pl.program_id(0) == 0)
    def _():
        for s in range(seqs):
            xt[s] = x[s].T

    def grad(source, lo, hi):
        total = nn(xt[0, :, lo:hi], source[0, lo:hi])
        for s in range(1, seqs):
            total = total + nn(xt[s, :, lo:hi], source[s, lo:hi])
        return total.astype(BF16)

    def bias(source, lo, hi):
        total = colsum(source[0, lo:hi].astype(F32))
        for s in range(1, seqs):
            total = total + colsum(source[s, lo:hi].astype(F32))
        return total

    for i, (source, lo, hi) in enumerate([
        (dqw, 0, WORDS), (dqe, 0, WORDS), (dqw, WORDS, length), (dqe, WORDS, length),
        (dk, 0, length), (dv, 0, length),
    ]):
        dw[i] = grad(source, lo, hi)
        if i != 4:
            sums[i:i + 1] = bias(source, lo, hi)


def qkv_grads(x, dqw, dqe, dk, dv, cols=256):
    seqs, length, width = x.shape
    part = pl.BlockSpec((seqs, length, cols), lambda j: (0, 0, j))
    return pl.pallas_call(
        qkv_grads_kernel,
        grid=(width // cols,),
        in_specs=[pl.BlockSpec((seqs, length, width), lambda j: (0, 0, 0), pipeline_mode=pl.Buffered(1))]
        + [part] * 4,
        out_specs=[
            pl.BlockSpec((6, width, cols), lambda j: (0, 0, j)),
            pl.BlockSpec((8, cols), lambda j: (0, j)),
        ],
        out_shape=[
            jax.ShapeDtypeStruct((6, width, width), BF16),
            jax.ShapeDtypeStruct((8, width), F32),
        ],
        scratch_shapes=[pltpu.VMEM((seqs, width, length), BF16)],
        compiler_params=vmem(60),
        name="qkv_grads",
    )(x, dqw, dqe, dk, dv)

MESH = pl.DeviceIdType.MESH
UNIT = 384


def place():
    d = lax.axis_index("dp")
    f = lax.axis_index("fsdp")
    bits = {"core": d % 2, "y": (d // 2) % 2, "z0": (d // 4) % 2, "z1": (d // 8) % 2, "x": f}
    peers = {"x": {"fsdp": 1 - f}}
    for name, size in (("core", 1), ("y", 2), ("z0", 4), ("z1", 8)):
        peers[name] = {"dp": d + size - 2 * size * bits[name]}
    return bits, peers


def greet(peers, names):
    barrier = pltpu.get_barrier_semaphore()
    for name in names:
        pl.semaphore_signal(barrier, inc=1, device_id=peers[name], device_id_type=MESH)
    pl.semaphore_wait(barrier, len(names))


def gather_project_kernel(*refs, units):
    own = refs[:9]
    small, x = refs[9:11]
    w6, wo, wi, wd, wide, ib, qw, qe, keys, vals, xt = refs[11:22]
    wv, table, qv, xt_held, send, recv, local, small_sem, q_sem = refs[22:]
    bits, peers = place()
    f, c = bits["x"], bits["core"]
    piece = UNIT // 8
    n = len(units)
    seqs, length, width = x.shape

    def load(u):
        i, kind, k = units[u]
        if kind == "wi":
            src = own[i].at[:, k * width:(k + 1) * width]
        else:
            src = own[i].at[k * UNIT:(k + 1) * UNIT]
        return pltpu.make_async_copy(src, wv.at[u, f], local.at[u])

    def store(u):
        i, kind, k = units[u]
        if kind == "w6":
            dst = w6.at[i]
        elif kind == "wo":
            dst = wo
        elif kind == "wi":
            dst = wi.at[:, :, k * width:(k + 1) * width]
        else:
            dst = wd.at[:, k]
        return pltpu.make_async_copy(wv.at[u], dst, local.at[u])

    small_in = pltpu.make_async_copy(small, table.at[f], small_sem.at[2])
    small_in.start()
    for u in range(n):
        load(u).start()
    greet(peers, ("x", "y", "z0", "core"))

    def remote(u, stage, half, rows, size, peer):
        here = wv.at[u, half, pl.ds(pl.multiple_of(rows, 16), size)]
        return pltpu.make_async_remote_copy(
            src_ref=here, dst_ref=here, send_sem=send.at[u, stage], recv_sem=recv.at[u, stage],
            device_id=peers[peer], device_id_type=MESH,
        )

    def copy(u, stage):
        first, second = ("y", "z0") if u % 2 == 0 else ("z0", "y")
        a, b = bits[first], bits[second]
        mine = (c * 4 + b * 2 + a) * piece
        pair = (c * 4 + b * 2) * piece
        away = (c * 4 + (1 - b) * 2) * piece
        if stage == 0:
            return remote(u, 0, f, mine, piece, "x")
        if stage == 1:
            return remote(u, 1, 1 - f, mine, piece, first)
        if stage == 2:
            return remote(u, 2, 1 - f, pair, 2 * piece, second)
        return remote(u, stage, 1 - f, pair if stage == 3 else away, 2 * piece, "core")

    small_in.wait()
    small_copy = pltpu.make_async_remote_copy(
        src_ref=table.at[f], dst_ref=table.at[f], send_sem=small_sem.at[0], recv_sem=small_sem.at[1],
        device_id=peers["x"], device_id_type=MESH,
    )
    small_copy.start()
    for u in range(n):
        load(u).wait()
        copy(u, 0).start()

    def fill_small():
        small_copy.wait_recv()
        half = table.shape[2]
        for s in range(2):
            wide[:, s * half:(s + 1) * half] = table[s].astype(F32)
            for r in range(4):
                ib[:, (4 * s + r) * half:(4 * s + r + 1) * half] = table[s, 12 + r:13 + r].astype(F32)

    cols = 256
    scale = HD ** -0.5

    def project(i):
        lo, hi = ((0, WORDS), (0, WORDS), (WORDS, length), (WORDS, length), (0, length), (0, length))[i]
        slot = (0, 1, 0, 1, 2, 3)[i]

        def tile(j, carry):
            at = pl.ds(pl.multiple_of(j * cols, cols), cols)
            w = wv[i, :, :, at].reshape(width, cols)
            for s in range(seqs):
                total = nn(x[s, lo:hi], w)
                if i != 4:
                    total = total + wide[i:i + 1, at]
                total = total.astype(BF16)
                if i < 4:
                    total = (total * scale).astype(BF16)
                qv[slot, s, lo:hi, at] = total
            return carry

        lax.fori_loop(0, width // cols, tile, 0)

    xt_out = pltpu.make_async_copy(xt_held, xt, q_sem.at[4])

    def q_out(slot):
        return pltpu.make_async_copy(qv.at[slot], (qw, qe, keys, vals)[slot], q_sem.at[slot])

    lag1, lag2, lag3 = 2, 4, 5
    for t in range(n + lag3):
        if t < n:
            copy(t, 0).wait_recv()
            copy(t, 1).start()
        if 0 <= t - lag1 < n:
            copy(t - lag1, 1).wait_recv()
            copy(t - lag1, 2).start()
            copy(t - lag1, 3).start()
        if 0 <= t - lag2 < n:
            copy(t - lag2, 2).wait_recv()
            copy(t - lag2, 4).start()
        if t == 1:
            for s in range(seqs):
                xt_held[s] = x[s].T
            xt_out.start()
        if t == 2:
            fill_small()
        done = t - lag3
        if 0 <= done < n:
            copy(done, 3).wait_recv()
            copy(done, 4).wait_recv()
            store(done).start()
        if 0 <= done < 6:
            project(done)
            if done >= 2:
                q_out(done - 2).start()
    for u in range(n):
        for stage in range(5):
            copy(u, stage).wait_send()
        store(u).wait()
    small_copy.wait_send()
    for slot in range(4):
        q_out(slot).wait()
    xt_out.wait()


def gather_project(own, small, x):
    units = [(i, "w6", 0) for i in range(6)] + [(6, "wo", 0)]
    for k in range(4):
        units += [(7, "wi", k), (8, "wd", k)]
    n = len(units)
    seqs, length, width = x.shape
    ff = own[7].shape[1]
    hbm = pl.BlockSpec(memory_space=pltpu.MemorySpace.HBM)
    vm = pl.BlockSpec(memory_space=pltpu.VMEM)
    q = jax.ShapeDtypeStruct(x.shape, BF16)
    w6, wo, wi, wd, wide, ib, qw, qe, keys, vals, xt = pl.pallas_call(
        functools.partial(gather_project_kernel, units=units),
        in_specs=[hbm] * 10 + [vm],
        out_specs=[hbm] * 4 + [vm] * 2 + [hbm] * 5,
        out_shape=[
            jax.ShapeDtypeStruct((6, 2, UNIT, width), BF16),
            jax.ShapeDtypeStruct((2, UNIT, width), BF16),
            jax.ShapeDtypeStruct((2, UNIT, ff), BF16),
            jax.ShapeDtypeStruct((2, 4, UNIT, width), BF16),
            jax.ShapeDtypeStruct((16, width), F32),
            jax.ShapeDtypeStruct((1, ff), F32),
            q, q, q, q,
            jax.ShapeDtypeStruct((seqs, width, length), BF16),
        ],
        scratch_shapes=[
            pltpu.VMEM((n, 2, UNIT, width), BF16),
            pltpu.VMEM((2,) + small.shape, small.dtype),
            pltpu.VMEM((4,) + x.shape, BF16),
            pltpu.VMEM((seqs, width, length), BF16),
            pltpu.SemaphoreType.DMA((n, 5)),
            pltpu.SemaphoreType.DMA((n, 5)),
            pltpu.SemaphoreType.DMA((n,)),
            pltpu.SemaphoreType.DMA((3,)),
            pltpu.SemaphoreType.DMA((5,)),
        ],
        compiler_params=pltpu.CompilerParams(
            collective_id=0, has_side_effects=True, vmem_limit_bytes=60 * 1024 * 1024
        ),
        name="gather_project",
    )(*own, small, x)
    return (w6.reshape(6, width, width), wo.reshape(width, width), wi.reshape(width, ff),
            wd.reshape(ff, width), wide, ib, qw, qe, keys, vals, xt)


def widen_kernel(g, *refs):
    outs = refs[:9]
    stage, sem = refs[9:]
    n = g.shape[0]
    width = g.shape[2]
    slots = stage.shape[0]

    def out(u):
        if u < 4:
            dst = outs[0].at[:, u * width:(u + 1) * width]
        elif u < 8:
            dst = outs[1].at[(u - 4) * UNIT:(u - 3) * UNIT]
        else:
            dst = outs[u - 6]
        return pltpu.make_async_copy(stage.at[u % slots], dst, sem.at[u % slots])

    for u in range(n):
        if u >= slots:
            out(u - slots).wait()
        stage[u % slots] = g[u].astype(F32)
        out(u).start()
    for u in range(n - slots, n):
        out(u).wait()


def widen(g):
    n, share, width = g.shape
    hbm = pl.BlockSpec(memory_space=pltpu.MemorySpace.HBM)
    square = jax.ShapeDtypeStruct((share, width), F32)
    return pl.pallas_call(
        widen_kernel,
        in_specs=[pl.BlockSpec(memory_space=pltpu.VMEM)],
        out_specs=[hbm] * 9,
        out_shape=[
            jax.ShapeDtypeStruct((share, 4 * width), F32),
            jax.ShapeDtypeStruct((4 * share, width), F32),
        ] + [square] * 7,
        scratch_shapes=[pltpu.VMEM((4, share, width), F32), pltpu.SemaphoreType.DMA((4,))],
        compiler_params=vmem(60),
        name="widen",
    )(g)


STAGES = ("core", "x", "y", "z0", "z1")
PAIRS_END = 12
UNITS_END = 18
STEPS = 24


class Reduction:
    def __init__(self, own, from_core, from_x, from_y, from_z0, from_z1, full, send, recv, peers, bits):
        self.own, self.full = own, full
        self.got = (from_core, from_x, from_y, from_z0, from_z1)
        self.send, self.recv, self.peers = send, recv, peers
        f = self.f = bits["x"]
        self.mine = pl.multiple_of(bits["core"] * UNIT, UNIT)
        self.theirs = pl.multiple_of((1 - bits["core"]) * UNIT, UNIT)
        y0 = self.y0 = bits["y"] * 192
        z0 = self.z0 = y0 + bits["z0"] * 96
        z1 = self.z1 = z0 + bits["z1"] * 48
        away = {
            1: ((1 - f) * UNIT, UNIT),
            2: (f * UNIT + (1 - bits["y"]) * 192, 192),
            3: (f * UNIT + y0 + (1 - bits["z0"]) * 96, 96),
            4: (f * UNIT + z0 + (1 - bits["z1"]) * 48, 48),
        }
        self.away = away
        self.back = {5: (z1, 48, "z1"), 6: (z0, 96, "z0"), 7: (y0, 192, "y"), 8: (0, UNIT, "core")}

    def rows(self, start, size):
        return pl.ds(pl.multiple_of(start, 16), size)

    def remote(self, u, stage, src, dst, peer):
        return pltpu.make_async_remote_copy(
            src_ref=src, dst_ref=dst, send_sem=self.send.at[u, stage], recv_sem=self.recv.at[u, stage],
            device_id=self.peers[peer], device_id_type=MESH,
        )

    def first(self, u, unit):
        return self.remote(u, 0, unit.at[:, pl.ds(self.theirs, UNIT)], self.got[0].at[u], "core")

    def copy(self, u, stage):
        if stage < 5:
            start, size = self.away[stage]
            src = self.own.at[u, self.rows(start, size)]
            return self.remote(u, stage, src, self.got[stage].at[u], STAGES[stage])
        start, size, peer = self.back[stage]
        here = self.full.at[u, self.rows(start, size), pl.ds(self.mine, UNIT)]
        return self.remote(u, stage, here, here, peer)

    def add(self, u, start, size, got):
        here = self.rows(start, size)
        self.own[u, here] = (self.own[u, here].astype(F32) + got.astype(F32)).astype(BF16)

    def after(self, u, stage):
        f = self.f
        if stage < 4:
            self.copy(u, stage).wait_recv()
            start, size = {1: (0, UNIT), 2: (self.y0, 192), 3: (self.z0, 96)}[stage]
            self.add(u, f * UNIT + start, size, self.got[stage][u])
            self.copy(u, stage + 1).start()
        elif stage == 4:
            self.copy(u, 4).wait_recv()
            here = self.rows(f * UNIT + self.z1, 48)
            self.full[u, self.rows(self.z1, 48), pl.ds(self.mine, UNIT)] = (
                self.own[u, here].astype(F32) + self.got[4][u].astype(F32)
            ).astype(BF16)
            self.copy(u, 5).start()
        elif stage < 8:
            self.copy(u, stage).wait_recv()
            self.copy(u, stage + 1).start()
        else:
            self.copy(u, 8).wait_recv()


LAGS = {1: 2, 2: 3, 3: 4, 4: 5, 5: 6, 6: 7, 7: 8, 8: 9}
SMALL_FROM = 10


def backward_kernel(seg, qw, qe, k, v, o, g, lse, xt, w6, gpre, gi, gd, go, small_in,
                    dx, out, small_out,
                    bias, grads, unit, full, own, from_core, from_x, from_y, from_z0, from_z1,
                    small_sum, small_got, send, recv, local, small_send, small_recv, *, step):
    i = pl.program_id(0)
    bits, peers = place()
    red = Reduction(own, from_core, from_x, from_y, from_z0, from_z1, full, send, recv, peers, bits)
    ready = gi.shape[0] + gd.shape[0] + go.shape[0]
    total = ready + 6
    seqs = xt.shape[0]
    width = xt.shape[1]
    length = xt.shape[2]
    sources = ((gi, 0), (gd, gi.shape[0]), (go, gi.shape[0] + gd.shape[0]))

    def load(g, n, u):
        return pltpu.make_async_copy(g.at[n, :, pl.ds(red.mine, UNIT)], own.at[u], local.at[u])

    def out_copy(u):
        return pltpu.make_async_copy(full.at[u], out.at[u], local.at[u])

    def small_copy(s):
        return pltpu.make_async_remote_copy(
            src_ref=small_sum.at[s], dst_ref=small_got.at[s], send_sem=small_send.at[s],
            recv_sem=small_recv.at[s], device_id=peers[STAGES[s]], device_id_type=MESH,
        )

    @pl.when(i == 0)
    def _():
        greet(peers, STAGES)
        small_sum[0] = small_in[...]
        for source, base in sources:
            def begin(n, carry, source=source, base=base):
                red.first(base + n, source.at[n]).start()
                load(source, n, base + n).start()
                return carry
            lax.fori_loop(0, source.shape[0], begin, 0)

    def comm_step(t, carry):
        @pl.when(t < total)
        def _():
            red.first(t, gi.at[0]).wait_recv()

            @pl.when(t < ready)
            def _():
                load(gi, 0, t).wait()
            for n in range(2):
                red.add(t, n * UNIT, UNIT, from_core[t, n * UNIT:(n + 1) * UNIT])
            red.copy(t, 1).start()

        for stage, lag in LAGS.items():
            @pl.when(jnp.logical_and(t >= lag, t < total + lag))
            def _(stage=stage, lag=lag):
                red.after(t - lag, stage)
                if stage == 8:
                    out_copy(t - lag).start()

        for s in range(5):
            @pl.when(t == SMALL_FROM + s)
            def _(s=s):
                small_copy(s).wait_recv()
                value = small_sum[s] + small_got[s]
                if s < 4:
                    small_sum[s + 1] = value
                    small_copy(s + 1).start()
                else:
                    small_out[...] = value
        return carry

    @pl.when(jnp.logical_and(i < PAIRS_END, i % 6 == 0))
    def _():
        bias[...] = document_bias(seg[0])

    @pl.when(i < PAIRS_END)
    def _():
        s = i // 6
        at = pl.ds(pl.multiple_of((i % 6) * 2 * HD, 2 * HD), 2 * HD)

        def put(slot, lo, n, value):
            grads[slot, s, pl.ds(lo, n), at] = value

        attend_back_pair(qw, qe, k, v, o, g, lse, bias, put, step)

    for n in range(6):
        @pl.when(i == PAIRS_END + n)
        def _(n=n):
            u = ready + n
            slot = (0, 1, 0, 1, 2, 3)[n]
            lo, hi = ((0, WORDS), (0, WORDS), (WORDS, length), (WORDS, length), (0, length), (0, length))[n]
            buf = unit.at[n % 2]
            if n >= 2:
                red.first(u - 2, buf).wait_send()

            def tile(j, carry):
                cols = pl.ds(pl.multiple_of(j * 256, 256), 256)
                value = nn(xt[0, :, lo:hi], grads[slot, 0, lo:hi, cols])
                for s in range(1, seqs):
                    value = value + nn(xt[s, :, lo:hi], grads[slot, s, lo:hi, cols])
                buf[:, cols] = value.astype(BF16)
                if n != 4:
                    column = colsum(grads[slot, 0, lo:hi, cols].astype(F32))
                    for s in range(1, seqs):
                        column = column + colsum(grads[slot, s, lo:hi, cols].astype(F32))
                    small_sum[0, 8 + n:9 + n, cols] = column
                return carry

            lax.fori_loop(0, width // 256, tile, 0)
            red.first(u, buf).start()
            own[u] = buf[:, pl.ds(red.mine, UNIT)]
            if n == 5:
                small_copy(0).start()

    @pl.when(i >= UNITS_END)
    def _():
        s = i % 2

        def grad(slot, lo, hi, n):
            return nt(grads[slot, s, lo:hi], w6[n])

        for lo, hi, a, b in ((0, WORDS, 0, 1), (WORDS, length, 2, 3)):
            dx[0, lo:hi] = (
                gpre[0, lo:hi] + grad(0, lo, hi, a) + grad(1, lo, hi, b)
                + grad(2, lo, hi, 4) + grad(3, lo, hi, 5)
            )

    @pl.when(i % 2 == 1)
    def _():
        comm_step(i // 2, 0)

    @pl.when(i == STEPS - 1)
    def _():
        lax.fori_loop(STEPS // 2, total + 9, comm_step, 0)

        def drain(u, carry):
            @pl.when(jnp.logical_or(u < ready, u >= ready + 4))
            def _():
                red.first(u, gi.at[0]).wait_send()
            for stage in range(1, 9):
                red.copy(u, stage).wait_send()
            out_copy(u).wait()
            return carry

        lax.fori_loop(0, total, drain, 0)
        for s in range(5):
            small_copy(s).wait_send()


def backward(qw, qe, k, v, seg, o, g, lse, xt, w6, gpre, units, small, step=256):
    seqs, length, width = k.shape
    gi, gd, go = units
    total = gi.shape[0] + gd.shape[0] + go.shape[0] + 6
    hbm = pl.BlockSpec(memory_space=pltpu.MemorySpace.HBM)
    vm = pl.BlockSpec(memory_space=pltpu.VMEM)

    def pair(i):
        return jnp.minimum(i, PAIRS_END - 1)

    def late(i):
        return jnp.maximum(i - UNITS_END, 0)

    spec = pl.BlockSpec((1, length, 2 * HD), lambda i: (pair(i) // 6, 0, pair(i) % 6))
    part = pl.BlockSpec((1, length, 256), lambda i: (late(i) % 2, 0, late(i) // 2))
    return pl.pallas_call(
        functools.partial(backward_kernel, step=step),
        grid=(STEPS,),
        in_specs=[
            pl.BlockSpec((1, 1, length), lambda i: (pair(i) // 6, 0, 0)),
            spec, spec, spec, spec, spec, spec,
            pl.BlockSpec((1, 1, 2, length), lambda i: (pair(i) // 6, pair(i) % 6, 0, 0)),
            pl.BlockSpec((seqs, width, length), lambda i: (0, 0, 0), pipeline_mode=pl.Buffered(1)),
            pl.BlockSpec((6, 256, width), lambda i: (0, late(i) // 2, 0), pipeline_mode=pl.Buffered(1)),
            part, hbm, hbm, hbm,
            pl.BlockSpec(small.shape, lambda i: (0, 0), pipeline_mode=pl.Buffered(1)),
        ],
        out_specs=[part, hbm, vm],
        out_shape=[
            jax.ShapeDtypeStruct((seqs, length, width), F32),
            jax.ShapeDtypeStruct((total, UNIT, width), BF16),
            jax.ShapeDtypeStruct(small.shape, F32),
        ],
        scratch_shapes=[
            pltpu.VMEM((length, length), F32),
            pltpu.VMEM((4, seqs, length, width), BF16),
            pltpu.VMEM((2, width, width), BF16),
            pltpu.VMEM((total, UNIT, width), BF16),
            pltpu.VMEM((total, 2 * UNIT, UNIT), BF16),
            pltpu.VMEM((total, 2 * UNIT, UNIT), BF16),
            pltpu.VMEM((total, 384, UNIT), BF16),
            pltpu.VMEM((total, 192, UNIT), BF16),
            pltpu.VMEM((total, 96, UNIT), BF16),
            pltpu.VMEM((total, 48, UNIT), BF16),
            pltpu.VMEM((5,) + small.shape, F32),
            pltpu.VMEM((5,) + small.shape, F32),
            pltpu.SemaphoreType.DMA((total, 9)),
            pltpu.SemaphoreType.DMA((total, 9)),
            pltpu.SemaphoreType.DMA((total,)),
            pltpu.SemaphoreType.DMA((5,)),
            pltpu.SemaphoreType.DMA((5,)),
        ],
        compiler_params=pltpu.CompilerParams(
            collective_id=1, has_side_effects=True, vmem_limit_bytes=67043328,
        ),
        name="backward",
    )(seg[:, None, :], qw, qe, k, v, o, g, lse, xt, w6, gpre, gi, gd, go, small)


def local(
    inputs, segments,
    query_wordword, query_wordent, query_entword, query_entent,
    bias_wordword, bias_wordent, bias_entword, bias_entent,
    key_weight, value_weight, value_bias, out_weight, out_bias,
    gain_attn, shift_attn, inner_weight, inner_bias, down_weight, down_bias,
    gain_ffn, shift_ffn, cotangent, *, dp, fsdp,
):
    seqs, length, width = inputs.shape
    share = width // fsdp
    ff = inner_weight.shape[1]
    paired = dp == 16 and fsdp == 2

    def gather_all(value):
        return lax.all_gather(value, "fsdp", axis=0, tiled=True)

    vectors = {
        0: bias_wordword, 1: bias_wordent, 2: bias_entword, 3: bias_entent, 5: value_bias,
        6: out_bias, 7: gain_attn, 8: shift_attn, 9: down_bias, 10: gain_ffn, 11: shift_ffn,
    }
    for n in range(4):
        vectors[12 + n] = inner_bias[n * share:(n + 1) * share]
    place_row = lax.broadcasted_iota(jnp.int32, (16, share), 0)
    packed = jnp.zeros((16, share), BF16)
    for n, vector in vectors.items():
        packed = jnp.where(place_row == n, vector[None, :], packed)
    own = (query_wordword, query_wordent, query_entword, query_entent, key_weight, value_weight,
           out_weight, inner_weight, down_weight)
    if paired:
        w6, wo, wi, wd, wide, ib, qw, qe, keys, vals, xt = gather_project(own, packed, inputs)
    else:
        w6 = jnp.stack([gather_all(w) for w in own[:6]])
        wo, wi, wd = [gather_all(w) for w in own[6:]]
        table = lax.all_gather(packed, "fsdp", axis=0)
        wide = table.transpose(1, 0, 2).reshape(16, width).astype(F32)
        ib = table[:, 12:].reshape(1, ff).astype(F32)
        qw, qe, keys, vals = project(inputs, w6, wide)
    ctx, lse = attend(qw, qe, keys, vals, segments)

    def flat(value):
        return value.reshape(seqs * length, width)

    ctx_rows = flat(ctx)
    out, gpre, hl, act, gu, gfed, gatt, gctx, sums = middle(
        flat(inputs), ctx_rows, flat(cotangent), wo, wi, wd, wide, ib)
    units = ffn_grads(hl, gu, act, gfed, ctx_rows, gatt)
    gctx = gctx.reshape(inputs.shape)
    gpre = gpre.reshape(inputs.shape)
    f = lax.axis_index("fsdp")

    if paired:
        grad_inputs, grads, totals = backward(
            qw, qe, keys, vals, segments, ctx, gctx, lse, xt, w6, gpre, units, sums)
        g_wi, g_wd, g_wo, *g6 = widen(grads)
    else:
        dqw, dqe, dk, dv = attend_back(qw, qe, keys, vals, segments, ctx, gctx, lse)
        grad_inputs = input_grads(dqw, dqe, dk, dv, w6, gpre)
        dw6, qsums = qkv_grads(inputs, dqw, dqe, dk, dv)

        def shared(grad):
            part = lax.psum_scatter(grad, "fsdp", scatter_dimension=0, tiled=True)
            return lax.psum(part, "dp").astype(F32)

        g_wi = shared(units[0].transpose(1, 0, 2).reshape(width, ff))
        g_wd = shared(units[1].reshape(4, 2, width // 2, width).transpose(1, 0, 2, 3).reshape(ff, width))
        g_wo = shared(units[2][0])
        g6 = [shared(dw6[i]) for i in range(6)]
        totals = lax.psum(jnp.concatenate([sums[:8], qsums, sums[16:]]), ("dp", "fsdp"))

    mine = lax.dynamic_slice_in_dim(totals[:16], f * share, share, axis=1)
    g_ib = lax.dynamic_slice_in_dim(totals[16:20].reshape(ff), f * (ff // fsdp), ff // fsdp)
    return (
        out.reshape(inputs.shape), grad_inputs,
        g6[0], g6[1], g6[2], g6[3],
        mine[8], mine[9], mine[10], mine[11],
        g6[4], g6[5], mine[13],
        g_wo, mine[OUT_BIAS], mine[GAIN_ATTN], mine[SHIFT_ATTN],
        g_wi, g_ib, g_wd, mine[DOWN_BIAS], mine[GAIN_FFN], mine[SHIFT_FFN],
    )


def solution(mesh):
    rows = P(("dp", "fsdp"), None, None)
    mat = P("fsdp", None)
    vec = P("fsdp")
    params = (mat,) * 4 + (vec,) * 4 + (mat, mat, vec, mat, vec, vec, vec, mat, vec, mat, vec, vec, vec)
    return jax.shard_map(
        functools.partial(local, dp=mesh.shape["dp"], fsdp=mesh.shape["fsdp"]),
        mesh=mesh,
        in_specs=(rows, P(("dp", "fsdp"), None)) + params + (rows,),
        out_specs=(rows, rows) + params,
        check_vma=False,
    )
```

```python
import functools
import jax
import jax.numpy as jnp
from jax import lax
from jax.experimental import pallas as pl
from jax.experimental.pallas import tpu as pltpu
from jax.sharding import PartitionSpec as P

HD = 64
WORDS = 512
norm_eps = 1e-12
F32 = jnp.float32
BF16 = jnp.bfloat16
MASKED = -1000000000.0


def nn(a, b):
    return lax.dot_general(a, b, (((1,), (0,)), ((), ())), preferred_element_type=F32)


def nt(a, b):
    return lax.dot_general(a, b, (((1,), (1,)), ((), ())), preferred_element_type=F32)


def vmem(mb):
    return pltpu.CompilerParams(vmem_limit_bytes=mb * 1024 * 1024)


def spans(total, size):
    return [(s, min(size, total - s)) for s in range(0, total, size)]


def project_kernel(x, w, b, qw, qe, k, v):
    words = x[0, :WORDS]
    ents = x[0, WORDS:]
    scale = HD ** -0.5

    def query(rows, i):
        return ((nn(rows, w[i]) + b[i:i + 1]).astype(BF16) * scale).astype(BF16)

    qw[0, :WORDS] = query(words, 0)
    qe[0, :WORDS] = query(words, 1)
    qw[0, WORDS:] = query(ents, 2)
    qe[0, WORDS:] = query(ents, 3)
    k[0] = nn(x[0], w[4]).astype(BF16)
    v[0] = (nn(x[0], w[5]) + b[5:6]).astype(BF16)


def project(x, w, b):
    seqs, length, width = x.shape
    cols = 256
    out = jax.ShapeDtypeStruct((seqs, length, width), BF16)
    spec = pl.BlockSpec((1, length, cols), lambda j, s: (s, 0, j))
    return pl.pallas_call(
        project_kernel,
        grid=(width // cols, seqs),
        in_specs=[
            pl.BlockSpec((1, length, width), lambda j, s: (s, 0, 0)),
            pl.BlockSpec((6, width, cols), lambda j, s: (0, 0, j)),
            pl.BlockSpec((16, cols), lambda j, s: (0, j)),
        ],
        out_specs=[spec] * 4,
        out_shape=[out] * 4,
        compiler_params=vmem(48),
        name="project",
    )(x, w, b)


def head_mask(h):
    lane = lax.broadcasted_iota(jnp.int32, (1, 2 * HD), 1)
    return jnp.where(lane // HD == h, 1.0, 0.0).astype(BF16)


def document_bias(seg):
    row = seg.astype(F32)
    col = jnp.broadcast_to(row, (8, row.shape[1])).T[:, :1]
    return jnp.where(col == row, 0.0, MASKED)


def attend_kernel(seg, qw, qe, k, v, o, lse, bias, *, step):
    @pl.when(pl.program_id(1) == 0)
    def _():
        bias[...] = document_bias(seg[0])

    length = k.shape[1]
    kp = k[0]
    vt = v[0].T
    for s, n in spans(length, step):
        parts = []
        for h in range(2):
            kh = kp * head_mask(h)
            st = jnp.concatenate(
                [nt(kh[:WORDS], qw[0, s:s + n]), nt(kh[WORDS:], qe[0, s:s + n])], axis=0
            ) + bias[:, s:s + n]
            peak = jnp.max(st, axis=0, keepdims=True)
            pt = jnp.exp(st - peak)
            total = jnp.sum(pt, axis=0, keepdims=True)
            ot = nn(vt[h * HD:(h + 1) * HD], pt.astype(BF16))
            parts.append(ot * (1.0 / total))
            lse[0, 0, h:h + 1, s:s + n] = peak + jnp.log(total)
        o[0, s:s + n] = jnp.concatenate(parts, axis=0).T.astype(BF16)


def attend(qw, qe, k, v, seg, step=640):
    seqs, length, width = k.shape
    pairs = width // (2 * HD)
    spec = pl.BlockSpec((1, length, 2 * HD), lambda s, h: (s, 0, h))
    return pl.pallas_call(
        functools.partial(attend_kernel, step=step),
        grid=(seqs, pairs),
        in_specs=[
            pl.BlockSpec((1, 1, length), lambda s, h: (s, 0, 0)),
            spec, spec, spec, spec,
        ],
        out_specs=[spec, pl.BlockSpec((1, 1, 2, length), lambda s, h: (s, h, 0, 0))],
        out_shape=[
            jax.ShapeDtypeStruct((seqs, length, width), BF16),
            jax.ShapeDtypeStruct((seqs, pairs, 2, length), F32),
        ],
        scratch_shapes=[pltpu.VMEM((length, length), F32)],
        compiler_params=vmem(48),
        name="attend",
    )(seg[:, None, :], qw, qe, k, v)


def attend_back_pair(qw, qe, k, v, o, g, lse, bias, put, step):
    length = k.shape[1]
    kp = k[0]
    kt = kp.T
    vp = v[0]
    scale = HD ** -0.5
    sums = None
    for s, n in spans(length, step):
        qws = qw[0, s:s + n]
        qes = qe[0, s:s + n]
        gs = g[0, s:s + n]
        prod = (gs.astype(F32) * o[0, s:s + n].astype(F32)).T
        dqw_parts = []
        dqe_parts = []
        for h in range(2):
            m = head_mask(h)
            kh = kp * m
            delta = jnp.sum(prod[h * HD:(h + 1) * HD], axis=0, keepdims=True)
            st = jnp.concatenate([nt(kh[:WORDS], qws), nt(kh[WORDS:], qes)], axis=0)
            pt = jnp.exp(st + bias[:, s:s + n] - lse[0, 0, h:h + 1, s:s + n])
            dpt = nt(vp * m, gs)
            dst = (pt * (dpt - delta)).astype(BF16)
            parts = (nn(pt.astype(BF16), gs * m), nn(dst[:WORDS], qws * m), nn(dst[WORDS:], qes * m))
            sums = parts if sums is None else tuple(a + b for a, b in zip(sums, parts))
            kth = kt[h * HD:(h + 1) * HD]
            dqw_parts.append(nn(kth[:, :WORDS], dst[:WORDS]))
            dqe_parts.append(nn(kth[:, WORDS:], dst[WORDS:]))
        put(0, s, n, (jnp.concatenate(dqw_parts, axis=0).T * scale).astype(BF16))
        put(1, s, n, (jnp.concatenate(dqe_parts, axis=0).T * scale).astype(BF16))
    put(2, 0, WORDS, sums[1].astype(BF16))
    put(2, WORDS, length - WORDS, sums[2].astype(BF16))
    put(3, 0, length, sums[0].astype(BF16))


def attend_back_kernel(seg, qw, qe, k, v, o, g, lse, dqw, dqe, dk, dv, bias, *, step):
    @pl.when(pl.program_id(1) == 0)
    def _():
        bias[...] = document_bias(seg[0])

    def put(slot, lo, n, value):
        (dqw, dqe, dk, dv)[slot][0, lo:lo + n] = value

    attend_back_pair(qw, qe, k, v, o, g, lse, bias, put, step)


def attend_back(qw, qe, k, v, seg, o, g, lse, step=256):
    seqs, length, width = k.shape
    pairs = width // (2 * HD)
    spec = pl.BlockSpec((1, length, 2 * HD), lambda s, h: (s, 0, h))
    out = jax.ShapeDtypeStruct((seqs, length, width), BF16)
    return pl.pallas_call(
        functools.partial(attend_back_kernel, step=step),
        grid=(seqs, pairs),
        in_specs=[
            pl.BlockSpec((1, 1, length), lambda s, h: (s, 0, 0)),
            spec, spec, spec, spec, spec, spec,
            pl.BlockSpec((1, 1, 2, length), lambda s, h: (s, h, 0, 0)),
        ],
        out_specs=[spec] * 4,
        out_shape=[out] * 4,
        scratch_shapes=[pltpu.VMEM((length, length), F32)],
        compiler_params=vmem(48),
        name="attend_back",
    )(seg[:, None, :], qw, qe, k, v, o, g, lse)


def norm_forward(values):
    center = values - jnp.mean(values, axis=-1, keepdims=True)
    scale = lax.rsqrt(jnp.mean(center * center, axis=-1, keepdims=True) + norm_eps)
    return center * scale, scale


def norm_backward(grad, normed, scale):
    first = jnp.mean(grad, axis=-1, keepdims=True)
    second = jnp.mean(grad * normed, axis=-1, keepdims=True)
    return scale * (grad - first - normed * second)


def gelu_pair(u):
    z = jnp.abs(u) * (0.5 ** 0.5)
    t = 1.0 / (1.0 + 0.3275911 * z)
    e = jnp.exp(u * u * -0.5)
    poly = 0.5 * 1.061405429
    poly = poly * t + 0.5 * -1.453152027
    poly = poly * t + 0.5 * 1.421413741
    poly = poly * t + 0.5 * -0.284496736
    poly = poly * t + 0.5 * 0.254829592
    tail = poly * t * e
    cdf = jnp.where(u < 0, tail, 1.0 - tail)
    return cdf, cdf + u * (e * 0.3989422804014327)


def colsum(v):
    return jnp.sum(v, axis=0, keepdims=True)


OUT_BIAS, GAIN_ATTN, SHIFT_ATTN, DOWN_BIAS, GAIN_FFN, SHIFT_FFN = range(6)


def middle_kernel(x, ctx, cot, wo, wi, wd, small, ib, out, gpre, hl, act, gu, gfed, gatt, gctx,
                  sums, slope, *, step):
    @pl.when(pl.program_id(0) == 0)
    def _():
        sums[...] = jnp.zeros_like(sums)

    def row(i):
        return small[6 + i:7 + i]

    ff = wi.shape[1]
    attended = nn(ctx[...], wo[...]) + row(OUT_BIAS)
    normed_attn, scale_attn = norm_forward(x[...].astype(F32) + attended)
    hidden = normed_attn * row(GAIN_ATTN) + row(SHIFT_ATTN)
    low = hidden.astype(BF16)
    hl[...] = low
    fed = jnp.broadcast_to(row(DOWN_BIAS), hidden.shape)
    for s, n in spans(ff, step):
        u = nn(low, wi[:, s:s + n]) + ib[:, s:s + n]
        cdf, grad = gelu_pair(u)
        slope[:, s:s + n] = grad
        a = (u * cdf).astype(BF16)
        act[:, s:s + n] = a
        fed = fed + nn(a, wd[s:s + n])
    normed_ffn, scale_ffn = norm_forward(hidden + fed)
    out[...] = (normed_ffn * row(GAIN_FFN) + row(SHIFT_FFN)).astype(BF16)
    gy = cot[...].astype(F32)
    sums[GAIN_FFN:GAIN_FFN + 1] += colsum(gy * normed_ffn)
    sums[SHIFT_FFN:SHIFT_FFN + 1] += colsum(gy)
    gsum = norm_backward(gy * row(GAIN_FFN), normed_ffn, scale_ffn)
    gf = gsum.astype(BF16)
    gfed[...] = gf
    sums[DOWN_BIAS:DOWN_BIAS + 1] += colsum(gf.astype(F32))
    ghid = gsum
    for s, n in spans(ff, step):
        d = nt(gf, wd[s:s + n]) * slope[:, s:s + n]
        sums[16 + s // n:17 + s // n] += colsum(d)
        d = d.astype(BF16)
        gu[:, s:s + n] = d
        ghid = ghid + nt(d, wi[:, s:s + n])
    sums[GAIN_ATTN:GAIN_ATTN + 1] += colsum(ghid * normed_attn)
    sums[SHIFT_ATTN:SHIFT_ATTN + 1] += colsum(ghid)
    gp = norm_backward(ghid * row(GAIN_ATTN), normed_attn, scale_attn)
    gpre[...] = gp
    ga = gp.astype(BF16)
    gatt[...] = ga
    sums[OUT_BIAS:OUT_BIAS + 1] += colsum(ga.astype(F32))
    gctx[...] = nt(ga, wo[...]).astype(BF16)


def middle(x, ctx, cot, wo, wi, wd, small, ib, rows=256, step=768):
    total, width = x.shape
    ff = wi.shape[1]

    def block(n):
        return pl.BlockSpec((rows, n), lambda i: (i, 0))

    def whole(*shape):
        return pl.BlockSpec(shape, lambda i: (0, 0), pipeline_mode=pl.Buffered(1))

    def out(n, dtype):
        return jax.ShapeDtypeStruct((total, n), dtype)

    return pl.pallas_call(
        functools.partial(middle_kernel, step=step),
        grid=(total // rows,),
        in_specs=[
            block(width), block(width), block(width),
            whole(width, width), whole(width, ff), whole(ff, width),
            whole(16, width), whole(1, ff),
        ],
        out_specs=[
            block(width), block(width), block(width), block(ff), block(ff),
            block(width), block(width), block(width),
            pl.BlockSpec((24, width), lambda i: (0, 0)),
        ],
        out_shape=[
            out(width, BF16), out(width, F32), out(width, BF16), out(ff, BF16), out(ff, BF16),
            out(width, BF16), out(width, BF16), out(width, BF16),
            jax.ShapeDtypeStruct((24, width), F32),
        ],
        scratch_shapes=[pltpu.VMEM((rows, ff), F32)],
        compiler_params=vmem(60),
        name="middle",
    )(x, ctx, cot, wo, wi, wd, small, ib)


def ffn_grads_kernel(hl, gu, act_lo, act_hi, gfed, ctx, gatt, dwi, dwd, dwo, hlt):
    @pl.when(pl.program_id(0) == 0)
    def _():
        hlt[...] = hl[...].T
        dwo[0] = nn(ctx[...].T, gatt[...]).astype(BF16)

    half = act_lo.shape[1]
    dwi[0] = nn(hlt[...], gu[...]).astype(BF16)
    dwd[0, :half] = nn(act_lo[...].T, gfed[...]).astype(BF16)
    dwd[0, half:] = nn(act_hi[...].T, gfed[...]).astype(BF16)


def ffn_grads(hl, gu, act, gfed, ctx, gatt):
    total, width = hl.shape
    count = gu.shape[1] // width
    half = width // 2

    def whole():
        return pl.BlockSpec((total, width), lambda j: (0, 0), pipeline_mode=pl.Buffered(1))

    square = pl.BlockSpec((1, width, width), lambda j: (j, 0, 0))
    return pl.pallas_call(
        ffn_grads_kernel,
        grid=(count,),
        in_specs=[
            whole(),
            pl.BlockSpec((total, width), lambda j: (0, j)),
            pl.BlockSpec((total, half), lambda j: (0, j)),
            pl.BlockSpec((total, half), lambda j: (0, count + j)),
            whole(), whole(), whole(),
        ],
        out_specs=[square, square, pl.BlockSpec((1, width, width), lambda j: (0, 0, 0))],
        out_shape=[
            jax.ShapeDtypeStruct((count, width, width), BF16),
            jax.ShapeDtypeStruct((count, width, width), BF16),
            jax.ShapeDtypeStruct((1, width, width), BF16),
        ],
        scratch_shapes=[pltpu.VMEM((width, total), BF16)],
        compiler_params=vmem(60),
        name="ffn_grads",
    )(hl, gu, act, act, gfed, ctx, gatt)


def input_grads_kernel(dqw, dqe, dk, dv, w, gpre, dx):
    dx[0, :WORDS] = (
        gpre[0, :WORDS] + nt(dqw[0, :WORDS], w[0]) + nt(dqe[0, :WORDS], w[1])
        + nt(dk[0, :WORDS], w[4]) + nt(dv[0, :WORDS], w[5])
    )
    dx[0, WORDS:] = (
        gpre[0, WORDS:] + nt(dqw[0, WORDS:], w[2]) + nt(dqe[0, WORDS:], w[3])
        + nt(dk[0, WORDS:], w[4]) + nt(dv[0, WORDS:], w[5])
    )


def input_grads(dqw, dqe, dk, dv, w, gpre):
    seqs, length, width = dqw.shape
    cols = 256
    full = pl.BlockSpec((1, length, width), lambda j, s: (s, 0, 0))
    part = pl.BlockSpec((1, length, cols), lambda j, s: (s, 0, j))
    return pl.pallas_call(
        input_grads_kernel,
        grid=(width // cols, seqs),
        in_specs=[full] * 4 + [pl.BlockSpec((6, cols, width), lambda j, s: (0, j, 0)), part],
        out_specs=part,
        out_shape=jax.ShapeDtypeStruct((seqs, length, width), F32),
        compiler_params=vmem(48),
        name="input_grads",
    )(dqw, dqe, dk, dv, w, gpre)


def qkv_grads_kernel(x, dqw, dqe, dk, dv, dw, sums, xt):
    seqs, length, width = x.shape

    @pl.when(pl.program_id(0) == 0)
    def _():
        for s in range(seqs):
            xt[s] = x[s].T

    def grad(source, lo, hi):
        total = nn(xt[0, :, lo:hi], source[0, lo:hi])
        for s in range(1, seqs):
            total = total + nn(xt[s, :, lo:hi], source[s, lo:hi])
        return total.astype(BF16)

    def bias(source, lo, hi):
        total = colsum(source[0, lo:hi].astype(F32))
        for s in range(1, seqs):
            total = total + colsum(source[s, lo:hi].astype(F32))
        return total

    for i, (source, lo, hi) in enumerate([
        (dqw, 0, WORDS), (dqe, 0, WORDS), (dqw, WORDS, length), (dqe, WORDS, length),
        (dk, 0, length), (dv, 0, length),
    ]):
        dw[i] = grad(source, lo, hi)
        if i != 4:
            sums[i:i + 1] = bias(source, lo, hi)


def qkv_grads(x, dqw, dqe, dk, dv, cols=256):
    seqs, length, width = x.shape
    part = pl.BlockSpec((seqs, length, cols), lambda j: (0, 0, j))
    return pl.pallas_call(
        qkv_grads_kernel,
        grid=(width // cols,),
        in_specs=[pl.BlockSpec((seqs, length, width), lambda j: (0, 0, 0), pipeline_mode=pl.Buffered(1))]
        + [part] * 4,
        out_specs=[
            pl.BlockSpec((6, width, cols), lambda j: (0, 0, j)),
            pl.BlockSpec((8, cols), lambda j: (0, j)),
        ],
        out_shape=[
            jax.ShapeDtypeStruct((6, width, width), BF16),
            jax.ShapeDtypeStruct((8, width), F32),
        ],
        scratch_shapes=[pltpu.VMEM((seqs, width, length), BF16)],
        compiler_params=vmem(60),
        name="qkv_grads",
    )(x, dqw, dqe, dk, dv)

MESH = pl.DeviceIdType.MESH
UNIT = 384


def place():
    d = lax.axis_index("dp")
    f = lax.axis_index("fsdp")
    bits = {"core": d % 2, "y": (d // 2) % 2, "z0": (d // 4) % 2, "z1": (d // 8) % 2, "x": f}
    peers = {"x": {"fsdp": 1 - f}}
    for name, size in (("core", 1), ("y", 2), ("z0", 4), ("z1", 8)):
        peers[name] = {"dp": d + size - 2 * size * bits[name]}
    return bits, peers


def greet(peers, names):
    barrier = pltpu.get_barrier_semaphore()
    for name in names:
        pl.semaphore_signal(barrier, inc=1, device_id=peers[name], device_id_type=MESH)
    pl.semaphore_wait(barrier, len(names))


def gather_project_kernel(*refs, units):
    own = refs[:9]
    small, x = refs[9:11]
    w6, wo, wi, wd, wide, ib, qw, qe, keys, vals, xt = refs[11:22]
    wv, table, qv, xt_held, send, recv, local, small_sem, q_sem = refs[22:]
    bits, peers = place()
    f, c = bits["x"], bits["core"]
    piece = UNIT // 8
    n = len(units)
    seqs, length, width = x.shape

    def load(u):
        i, kind, k = units[u]
        if kind == "wi":
            src = own[i].at[:, k * width:(k + 1) * width]
        else:
            src = own[i].at[k * UNIT:(k + 1) * UNIT]
        return pltpu.make_async_copy(src, wv.at[u, f], local.at[u])

    def store(u):
        i, kind, k = units[u]
        if kind == "w6":
            dst = w6.at[i]
        elif kind == "wo":
            dst = wo
        elif kind == "wi":
            dst = wi.at[:, :, k * width:(k + 1) * width]
        else:
            dst = wd.at[:, k]
        return pltpu.make_async_copy(wv.at[u], dst, local.at[u])

    small_in = pltpu.make_async_copy(small, table.at[f], small_sem.at[2])
    small_in.start()
    for u in range(n):
        load(u).start()
    greet(peers, ("x", "y", "z0", "core"))

    def remote(u, stage, half, rows, size, peer):
        here = wv.at[u, half, pl.ds(pl.multiple_of(rows, 16), size)]
        return pltpu.make_async_remote_copy(
            src_ref=here, dst_ref=here, send_sem=send.at[u, stage], recv_sem=recv.at[u, stage],
            device_id=peers[peer], device_id_type=MESH,
        )

    def copy(u, stage):
        first, second = ("y", "z0") if u % 2 == 0 else ("z0", "y")
        a, b = bits[first], bits[second]
        mine = (c * 4 + b * 2 + a) * piece
        pair = (c * 4 + b * 2) * piece
        away = (c * 4 + (1 - b) * 2) * piece
        if stage == 0:
            return remote(u, 0, f, mine, piece, "x")
        if stage == 1:
            return remote(u, 1, 1 - f, mine, piece, first)
        if stage == 2:
            return remote(u, 2, 1 - f, pair, 2 * piece, second)
        return remote(u, stage, 1 - f, pair if stage == 3 else away, 2 * piece, "core")

    small_in.wait()
    small_copy = pltpu.make_async_remote_copy(
        src_ref=table.at[f], dst_ref=table.at[f], send_sem=small_sem.at[0], recv_sem=small_sem.at[1],
        device_id=peers["x"], device_id_type=MESH,
    )
    small_copy.start()
    for u in range(n):
        load(u).wait()
        copy(u, 0).start()

    def fill_small():
        small_copy.wait_recv()
        half = table.shape[2]
        for s in range(2):
            wide[:, s * half:(s + 1) * half] = table[s].astype(F32)
            for r in range(4):
                ib[:, (4 * s + r) * half:(4 * s + r + 1) * half] = table[s, 12 + r:13 + r].astype(F32)

    cols = 256
    scale = HD ** -0.5

    def project(i):
        lo, hi = ((0, WORDS), (0, WORDS), (WORDS, length), (WORDS, length), (0, length), (0, length))[i]
        slot = (0, 1, 0, 1, 2, 3)[i]

        def tile(j, carry):
            at = pl.ds(pl.multiple_of(j * cols, cols), cols)
            w = wv[i, :, :, at].reshape(width, cols)
            for s in range(seqs):
                total = nn(x[s, lo:hi], w)
                if i != 4:
                    total = total + wide[i:i + 1, at]
                total = total.astype(BF16)
                if i < 4:
                    total = (total * scale).astype(BF16)
                qv[slot, s, lo:hi, at] = total
            return carry

        lax.fori_loop(0, width // cols, tile, 0)

    xt_out = pltpu.make_async_copy(xt_held, xt, q_sem.at[4])

    def q_out(slot):
        return pltpu.make_async_copy(qv.at[slot], (qw, qe, keys, vals)[slot], q_sem.at[slot])

    lag1, lag2, lag3 = 2, 4, 5
    for t in range(n + lag3):
        if t < n:
            copy(t, 0).wait_recv()
            copy(t, 1).start()
        if 0 <= t - lag1 < n:
            copy(t - lag1, 1).wait_recv()
            copy(t - lag1, 2).start()
            copy(t - lag1, 3).start()
        if 0 <= t - lag2 < n:
            copy(t - lag2, 2).wait_recv()
            copy(t - lag2, 4).start()
        if t == 1:
            for s in range(seqs):
                xt_held[s] = x[s].T
            xt_out.start()
        if t == 2:
            fill_small()
        done = t - lag3
        if 0 <= done < n:
            copy(done, 3).wait_recv()
            copy(done, 4).wait_recv()
            store(done).start()
        if 0 <= done < 6:
            project(done)
            if done >= 2:
                q_out(done - 2).start()
    for u in range(n):
        for stage in range(5):
            copy(u, stage).wait_send()
        store(u).wait()
    small_copy.wait_send()
    for slot in range(4):
        q_out(slot).wait()
    xt_out.wait()


def gather_project(own, small, x):
    units = [(i, "w6", 0) for i in range(6)] + [(6, "wo", 0)]
    for k in range(4):
        units += [(7, "wi", k), (8, "wd", k)]
    n = len(units)
    seqs, length, width = x.shape
    ff = own[7].shape[1]
    hbm = pl.BlockSpec(memory_space=pltpu.MemorySpace.HBM)
    vm = pl.BlockSpec(memory_space=pltpu.VMEM)
    q = jax.ShapeDtypeStruct(x.shape, BF16)
    w6, wo, wi, wd, wide, ib, qw, qe, keys, vals, xt = pl.pallas_call(
        functools.partial(gather_project_kernel, units=units),
        in_specs=[hbm] * 10 + [vm],
        out_specs=[hbm] * 4 + [vm] * 2 + [hbm] * 5,
        out_shape=[
            jax.ShapeDtypeStruct((6, 2, UNIT, width), BF16),
            jax.ShapeDtypeStruct((2, UNIT, width), BF16),
            jax.ShapeDtypeStruct((2, UNIT, ff), BF16),
            jax.ShapeDtypeStruct((2, 4, UNIT, width), BF16),
            jax.ShapeDtypeStruct((16, width), F32),
            jax.ShapeDtypeStruct((1, ff), F32),
            q, q, q, q,
            jax.ShapeDtypeStruct((seqs, width, length), BF16),
        ],
        scratch_shapes=[
            pltpu.VMEM((n, 2, UNIT, width), BF16),
            pltpu.VMEM((2,) + small.shape, small.dtype),
            pltpu.VMEM((4,) + x.shape, BF16),
            pltpu.VMEM((seqs, width, length), BF16),
            pltpu.SemaphoreType.DMA((n, 5)),
            pltpu.SemaphoreType.DMA((n, 5)),
            pltpu.SemaphoreType.DMA((n,)),
            pltpu.SemaphoreType.DMA((3,)),
            pltpu.SemaphoreType.DMA((5,)),
        ],
        compiler_params=pltpu.CompilerParams(
            collective_id=0, has_side_effects=True, vmem_limit_bytes=60 * 1024 * 1024
        ),
        name="gather_project",
    )(*own, small, x)
    return (w6.reshape(6, width, width), wo.reshape(width, width), wi.reshape(width, ff),
            wd.reshape(ff, width), wide, ib, qw, qe, keys, vals, xt)


def widen_kernel(g, *refs):
    outs = refs[:9]
    stage, sem = refs[9:]
    n = g.shape[0]
    width = g.shape[2]
    slots = stage.shape[0]

    def out(u):
        if u < 4:
            dst = outs[0].at[:, u * width:(u + 1) * width]
        elif u < 8:
            dst = outs[1].at[(u - 4) * UNIT:(u - 3) * UNIT]
        else:
            dst = outs[u - 6]
        return pltpu.make_async_copy(stage.at[u % slots], dst, sem.at[u % slots])

    for u in range(n):
        if u >= slots:
            out(u - slots).wait()
        stage[u % slots] = g[u].astype(F32)
        out(u).start()
    for u in range(n - slots, n):
        out(u).wait()


def widen(g):
    n, share, width = g.shape
    hbm = pl.BlockSpec(memory_space=pltpu.MemorySpace.HBM)
    square = jax.ShapeDtypeStruct((share, width), F32)
    return pl.pallas_call(
        widen_kernel,
        in_specs=[pl.BlockSpec(memory_space=pltpu.VMEM)],
        out_specs=[hbm] * 9,
        out_shape=[
            jax.ShapeDtypeStruct((share, 4 * width), F32),
            jax.ShapeDtypeStruct((4 * share, width), F32),
        ] + [square] * 7,
        scratch_shapes=[pltpu.VMEM((4, share, width), F32), pltpu.SemaphoreType.DMA((4,))],
        compiler_params=vmem(60),
        name="widen",
    )(g)


STAGES = ("core", "x", "y", "z0", "z1")
PAIRS_END = 12
UNITS_END = 18
STEPS = 24


class Reduction:
    def __init__(self, own, from_core, from_x, from_y, from_z0, from_z1, full, send, recv, peers, bits):
        self.own, self.full = own, full
        self.got = (from_core, from_x, from_y, from_z0, from_z1)
        self.send, self.recv, self.peers = send, recv, peers
        f = self.f = bits["x"]
        self.mine = pl.multiple_of(bits["core"] * UNIT, UNIT)
        self.theirs = pl.multiple_of((1 - bits["core"]) * UNIT, UNIT)
        y0 = self.y0 = bits["y"] * 192
        z0 = self.z0 = y0 + bits["z0"] * 96
        z1 = self.z1 = z0 + bits["z1"] * 48
        away = {
            1: ((1 - f) * UNIT, UNIT),
            2: (f * UNIT + (1 - bits["y"]) * 192, 192),
            3: (f * UNIT + y0 + (1 - bits["z0"]) * 96, 96),
            4: (f * UNIT + z0 + (1 - bits["z1"]) * 48, 48),
        }
        self.away = away
        self.back = {5: (z1, 48, "z1"), 6: (z0, 96, "z0"), 7: (y0, 192, "y"), 8: (0, UNIT, "core")}

    def rows(self, start, size):
        return pl.ds(pl.multiple_of(start, 16), size)

    def remote(self, u, stage, src, dst, peer):
        return pltpu.make_async_remote_copy(
            src_ref=src, dst_ref=dst, send_sem=self.send.at[u, stage], recv_sem=self.recv.at[u, stage],
            device_id=self.peers[peer], device_id_type=MESH,
        )

    def first(self, u, unit):
        return self.remote(u, 0, unit.at[:, pl.ds(self.theirs, UNIT)], self.got[0].at[u], "core")

    def copy(self, u, stage):
        if stage < 5:
            start, size = self.away[stage]
            src = self.own.at[u, self.rows(start, size)]
            return self.remote(u, stage, src, self.got[stage].at[u], STAGES[stage])
        start, size, peer = self.back[stage]
        here = self.full.at[u, self.rows(start, size), pl.ds(self.mine, UNIT)]
        return self.remote(u, stage, here, here, peer)

    def add(self, u, start, size, got):
        here = self.rows(start, size)
        self.own[u, here] = (self.own[u, here].astype(F32) + got.astype(F32)).astype(BF16)

    def after(self, u, stage):
        f = self.f
        if stage < 4:
            self.copy(u, stage).wait_recv()
            start, size = {1: (0, UNIT), 2: (self.y0, 192), 3: (self.z0, 96)}[stage]
            self.add(u, f * UNIT + start, size, self.got[stage][u])
            self.copy(u, stage + 1).start()
        elif stage == 4:
            self.copy(u, 4).wait_recv()
            here = self.rows(f * UNIT + self.z1, 48)
            self.full[u, self.rows(self.z1, 48), pl.ds(self.mine, UNIT)] = (
                self.own[u, here].astype(F32) + self.got[4][u].astype(F32)
            ).astype(BF16)
            self.copy(u, 5).start()
        elif stage < 8:
            self.copy(u, stage).wait_recv()
            self.copy(u, stage + 1).start()
        else:
            self.copy(u, 8).wait_recv()


LAGS = {1: 2, 2: 3, 3: 4, 4: 5, 5: 6, 6: 7, 7: 8, 8: 9}
SMALL_FROM = 10


def backward_kernel(seg, qw, qe, k, v, o, g, lse, xt, w6, gpre, gi, gd, go, small_in,
                    dx, out, small_out,
                    bias, grads, unit, full, own, from_core, from_x, from_y, from_z0, from_z1,
                    small_sum, small_got, send, recv, local, small_send, small_recv, *, step):
    i = pl.program_id(0)
    bits, peers = place()
    red = Reduction(own, from_core, from_x, from_y, from_z0, from_z1, full, send, recv, peers, bits)
    ready = gi.shape[0] + gd.shape[0] + go.shape[0]
    total = ready + 6
    seqs = xt.shape[0]
    width = xt.shape[1]
    length = xt.shape[2]
    sources = ((gi, 0), (gd, gi.shape[0]), (go, gi.shape[0] + gd.shape[0]))

    def load(g, n, u):
        return pltpu.make_async_copy(g.at[n, :, pl.ds(red.mine, UNIT)], own.at[u], local.at[u])

    def out_copy(u):
        return pltpu.make_async_copy(full.at[u], out.at[u], local.at[u])

    def small_copy(s):
        return pltpu.make_async_remote_copy(
            src_ref=small_sum.at[s], dst_ref=small_got.at[s], send_sem=small_send.at[s],
            recv_sem=small_recv.at[s], device_id=peers[STAGES[s]], device_id_type=MESH,
        )

    @pl.when(i == 0)
    def _():
        greet(peers, STAGES)
        small_sum[0] = small_in[...]
        for source, base in sources:
            def begin(n, carry, source=source, base=base):
                red.first(base + n, source.at[n]).start()
                load(source, n, base + n).start()
                return carry
            lax.fori_loop(0, source.shape[0], begin, 0)

    def comm_step(t, carry):
        @pl.when(t < total)
        def _():
            red.first(t, gi.at[0]).wait_recv()

            @pl.when(t < ready)
            def _():
                load(gi, 0, t).wait()
            for n in range(2):
                red.add(t, n * UNIT, UNIT, from_core[t, n * UNIT:(n + 1) * UNIT])
            red.copy(t, 1).start()

        for stage, lag in LAGS.items():
            @pl.when(jnp.logical_and(t >= lag, t < total + lag))
            def _(stage=stage, lag=lag):
                red.after(t - lag, stage)
                if stage == 8:
                    out_copy(t - lag).start()

        for s in range(5):
            @pl.when(t == SMALL_FROM + s)
            def _(s=s):
                small_copy(s).wait_recv()
                value = small_sum[s] + small_got[s]
                if s < 4:
                    small_sum[s + 1] = value
                    small_copy(s + 1).start()
                else:
                    small_out[...] = value
        return carry

    @pl.when(jnp.logical_and(i < PAIRS_END, i % 6 == 0))
    def _():
        bias[...] = document_bias(seg[0])

    @pl.when(i < PAIRS_END)
    def _():
        s = i // 6
        at = pl.ds(pl.multiple_of((i % 6) * 2 * HD, 2 * HD), 2 * HD)

        def put(slot, lo, n, value):
            grads[slot, s, pl.ds(lo, n), at] = value

        attend_back_pair(qw, qe, k, v, o, g, lse, bias, put, step)

    for n in range(6):
        @pl.when(i == PAIRS_END + n)
        def _(n=n):
            u = ready + n
            slot = (0, 1, 0, 1, 2, 3)[n]
            lo, hi = ((0, WORDS), (0, WORDS), (WORDS, length), (WORDS, length), (0, length), (0, length))[n]
            buf = unit.at[n % 2]
            if n >= 2:
                red.first(u - 2, buf).wait_send()

            def tile(j, carry):
                cols = pl.ds(pl.multiple_of(j * 256, 256), 256)
                value = nn(xt[0, :, lo:hi], grads[slot, 0, lo:hi, cols])
                for s in range(1, seqs):
                    value = value + nn(xt[s, :, lo:hi], grads[slot, s, lo:hi, cols])
                buf[:, cols] = value.astype(BF16)
                if n != 4:
                    column = colsum(grads[slot, 0, lo:hi, cols].astype(F32))
                    for s in range(1, seqs):
                        column = column + colsum(grads[slot, s, lo:hi, cols].astype(F32))
                    small_sum[0, 8 + n:9 + n, cols] = column
                return carry

            lax.fori_loop(0, width // 256, tile, 0)
            red.first(u, buf).start()
            own[u] = buf[:, pl.ds(red.mine, UNIT)]
            if n == 5:
                small_copy(0).start()

    @pl.when(i >= UNITS_END)
    def _():
        s = i % 2

        def grad(slot, lo, hi, n):
            return nt(grads[slot, s, lo:hi], w6[n])

        for lo, hi, a, b in ((0, WORDS, 0, 1), (WORDS, length, 2, 3)):
            dx[0, lo:hi] = (
                gpre[0, lo:hi] + grad(0, lo, hi, a) + grad(1, lo, hi, b)
                + grad(2, lo, hi, 4) + grad(3, lo, hi, 5)
            )

    @pl.when(i % 2 == 1)
    def _():
        comm_step(i // 2, 0)

    @pl.when(i == STEPS - 1)
    def _():
        lax.fori_loop(STEPS // 2, total + 9, comm_step, 0)

        def drain(u, carry):
            @pl.when(jnp.logical_or(u < ready, u >= ready + 4))
            def _():
                red.first(u, gi.at[0]).wait_send()
            for stage in range(1, 9):
                red.copy(u, stage).wait_send()
            out_copy(u).wait()
            return carry

        lax.fori_loop(0, total, drain, 0)
        for s in range(5):
            small_copy(s).wait_send()


def backward(qw, qe, k, v, seg, o, g, lse, xt, w6, gpre, units, small, step=256):
    seqs, length, width = k.shape
    gi, gd, go = units
    total = gi.shape[0] + gd.shape[0] + go.shape[0] + 6
    hbm = pl.BlockSpec(memory_space=pltpu.MemorySpace.HBM)
    vm = pl.BlockSpec(memory_space=pltpu.VMEM)

    def pair(i):
        return jnp.minimum(i, PAIRS_END - 1)

    def late(i):
        return jnp.maximum(i - UNITS_END, 0)

    spec = pl.BlockSpec((1, length, 2 * HD), lambda i: (pair(i) // 6, 0, pair(i) % 6))
    part = pl.BlockSpec((1, length, 256), lambda i: (late(i) % 2, 0, late(i) // 2))
    return pl.pallas_call(
        functools.partial(backward_kernel, step=step),
        grid=(STEPS,),
        in_specs=[
            pl.BlockSpec((1, 1, length), lambda i: (pair(i) // 6, 0, 0)),
            spec, spec, spec, spec, spec, spec,
            pl.BlockSpec((1, 1, 2, length), lambda i: (pair(i) // 6, pair(i) % 6, 0, 0)),
            pl.BlockSpec((seqs, width, length), lambda i: (0, 0, 0), pipeline_mode=pl.Buffered(1)),
            pl.BlockSpec((6, 256, width), lambda i: (0, late(i) // 2, 0), pipeline_mode=pl.Buffered(1)),
            part, hbm, hbm, hbm,
            pl.BlockSpec(small.shape, lambda i: (0, 0), pipeline_mode=pl.Buffered(1)),
        ],
        out_specs=[part, hbm, vm],
        out_shape=[
            jax.ShapeDtypeStruct((seqs, length, width), F32),
            jax.ShapeDtypeStruct((total, UNIT, width), BF16),
            jax.ShapeDtypeStruct(small.shape, F32),
        ],
        scratch_shapes=[
            pltpu.VMEM((length, length), F32),
            pltpu.VMEM((4, seqs, length, width), BF16),
            pltpu.VMEM((2, width, width), BF16),
            pltpu.VMEM((total, UNIT, width), BF16),
            pltpu.VMEM((total, 2 * UNIT, UNIT), BF16),
            pltpu.VMEM((total, 2 * UNIT, UNIT), BF16),
            pltpu.VMEM((total, 384, UNIT), BF16),
            pltpu.VMEM((total, 192, UNIT), BF16),
            pltpu.VMEM((total, 96, UNIT), BF16),
            pltpu.VMEM((total, 48, UNIT), BF16),
            pltpu.VMEM((5,) + small.shape, F32),
            pltpu.VMEM((5,) + small.shape, F32),
            pltpu.SemaphoreType.DMA((total, 9)),
            pltpu.SemaphoreType.DMA((total, 9)),
            pltpu.SemaphoreType.DMA((total,)),
            pltpu.SemaphoreType.DMA((5,)),
            pltpu.SemaphoreType.DMA((5,)),
        ],
        compiler_params=pltpu.CompilerParams(
            collective_id=1, has_side_effects=True, vmem_limit_bytes=67043328,
        ),
        name="backward",
    )(seg[:, None, :], qw, qe, k, v, o, g, lse, xt, w6, gpre, gi, gd, go, small)


def local(
    inputs, segments,
    query_wordword, query_wordent, query_entword, query_entent,
    bias_wordword, bias_wordent, bias_entword, bias_entent,
    key_weight, value_weight, value_bias, out_weight, out_bias,
    gain_attn, shift_attn, inner_weight, inner_bias, down_weight, down_bias,
    gain_ffn, shift_ffn, cotangent, *, dp, fsdp,
):
    seqs, length, width = inputs.shape
    share = width // fsdp
    ff = inner_weight.shape[1]
    paired = dp == 16 and fsdp == 2

    def gather_all(value):
        return lax.all_gather(value, "fsdp", axis=0, tiled=True)

    vectors = {
        0: bias_wordword, 1: bias_wordent, 2: bias_entword, 3: bias_entent, 5: value_bias,
        6: out_bias, 7: gain_attn, 8: shift_attn, 9: down_bias, 10: gain_ffn, 11: shift_ffn,
    }
    for n in range(4):
        vectors[12 + n] = inner_bias[n * share:(n + 1) * share]
    place_row = lax.broadcasted_iota(jnp.int32, (16, share), 0)
    packed = jnp.zeros((16, share), BF16)
    for n, vector in vectors.items():
        packed = jnp.where(place_row == n, vector[None, :], packed)
    own = (query_wordword, query_wordent, query_entword, query_entent, key_weight, value_weight,
           out_weight, inner_weight, down_weight)
    if paired:
        w6, wo, wi, wd, wide, ib, qw, qe, keys, vals, xt = gather_project(own, packed, inputs)
    else:
        w6 = jnp.stack([gather_all(w) for w in own[:6]])
        wo, wi, wd = [gather_all(w) for w in own[6:]]
        table = lax.all_gather(packed, "fsdp", axis=0)
        wide = table.transpose(1, 0, 2).reshape(16, width).astype(F32)
        ib = table[:, 12:].reshape(1, ff).astype(F32)
        qw, qe, keys, vals = project(inputs, w6, wide)
    ctx, lse = attend(qw, qe, keys, vals, segments)

    def flat(value):
        return value.reshape(seqs * length, width)

    ctx_rows = flat(ctx)
    out, gpre, hl, act, gu, gfed, gatt, gctx, sums = middle(
        flat(inputs), ctx_rows, flat(cotangent), wo, wi, wd, wide, ib)
    units = ffn_grads(hl, gu, act, gfed, ctx_rows, gatt)
    gctx = gctx.reshape(inputs.shape)
    gpre = gpre.reshape(inputs.shape)
    f = lax.axis_index("fsdp")

    if paired:
        grad_inputs, grads, totals = backward(
            qw, qe, keys, vals, segments, ctx, gctx, lse, xt, w6, gpre, units, sums)
        g_wi, g_wd, g_wo, *g6 = widen(grads)
    else:
        dqw, dqe, dk, dv = attend_back(qw, qe, keys, vals, segments, ctx, gctx, lse)
        grad_inputs = input_grads(dqw, dqe, dk, dv, w6, gpre)
        dw6, qsums = qkv_grads(inputs, dqw, dqe, dk, dv)

        def shared(grad):
            part = lax.psum_scatter(grad, "fsdp", scatter_dimension=0, tiled=True)
            return lax.psum(part, "dp").astype(F32)

        g_wi = shared(units[0].transpose(1, 0, 2).reshape(width, ff))
        g_wd = shared(units[1].reshape(4, 2, width // 2, width).transpose(1, 0, 2, 3).reshape(ff, width))
        g_wo = shared(units[2][0])
        g6 = [shared(dw6[i]) for i in range(6)]
        totals = lax.psum(jnp.concatenate([sums[:8], qsums, sums[16:]]), ("dp", "fsdp"))

    mine = lax.dynamic_slice_in_dim(totals[:16], f * share, share, axis=1)
    g_ib = lax.dynamic_slice_in_dim(totals[16:20].reshape(ff), f * (ff // fsdp), ff // fsdp)
    return (
        out.reshape(inputs.shape), grad_inputs,
        g6[0], g6[1], g6[2], g6[3],
        mine[8], mine[9], mine[10], mine[11],
        g6[4], g6[5], mine[13],
        g_wo, mine[OUT_BIAS], mine[GAIN_ATTN], mine[SHIFT_ATTN],
        g_wi, g_ib, g_wd, mine[DOWN_BIAS], mine[GAIN_FFN], mine[SHIFT_FFN],
    )


def solution(mesh):
    rows = P(("dp", "fsdp"), None, None)
    mat = P("fsdp", None)
    vec = P("fsdp")
    params = (mat,) * 4 + (vec,) * 4 + (mat, mat, vec, mat, vec, vec, vec, mat, vec, mat, vec, vec, vec)
    return jax.shard_map(
        functools.partial(local, dp=mesh.shape["dp"], fsdp=mesh.shape["fsdp"]),
        mesh=mesh,
        in_specs=(rows, P(("dp", "fsdp"), None)) + params + (rows,),
        out_specs=(rows, rows) + params,
        check_vma=False,
    )
```
